256 devices in a mesh: rows: 32 (over y, x, core), rhs: 8 (over z).
Axes of the slice: x: 4, y: 4, z: 8, core: 2. Of those that a mesh axis runs over, the one named last changes fastest.
Arguments:
- samples: float32 [524288, 16], P(('rows', 'rhs')), may hold values from -5 to 5
- freq_table: float32 [4096, 16], replicated, may hold values from -3 to 3
- feature_seeds: int32 [512], replicated, may hold values from 0 to 4095
- phases: float32 [512], replicated, may hold values from -3.140625 to 3.140625
- treatment_features: bfloat16 [524288, 512], P('rows', 'rhs'), may hold values from -2.5 to 2.5, as said below
Outputs:
- coefficients: float32 [512, 512], replicated
- fitted: float32 [524288, 512], P(('rows', 'rhs'))
The draws below stay inside these ranges and needn't reach their ends.
Inputs may be any that keep to these rules, and one draw needn't show every extreme that they name: `treatment_features`: treatment features depend on the instrument values.
All inputs are finite; a program needn't handle non-finite values.
Results may differ from the reference program's by a relative error of at most 0.0008.
The reference program's roundings to bfloat16 on the way count: a program that leaves them out, or rounds other values in their place, can miss the bound.
Values may be sent and summed in bfloat16 or wider, within the bound.
No kernel may reach another device: no remote copies, remote signals or barrier semaphores. Data moves between devices by JAX's collectives and lax.ppermute only.
A program may use at most 64 MiB of HBM per device.

```python
import jax
import jax.numpy as jnp
from jax import lax

M = 512
P_SIZE = 512
DX = 16
NFREQ = 4096
TOTAL = 524288


def joint_values(key):
    base = jax.random.fold_in(key, 7)
    values = jnp.clip(jax.random.normal(jax.random.fold_in(base, 1), (TOTAL, DX), jnp.float32), -5.0, 5.0)
    mixing = jax.random.normal(jax.random.fold_in(base, 2), (DX, P_SIZE), jnp.float32) * 0.4
    noise = jax.random.normal(jax.random.fold_in(base, 3), (TOTAL, P_SIZE), jnp.float32)
    targets = jnp.clip(jnp.tanh(jnp.dot(values, mixing)) + 0.3 * noise, -2.5, 2.5)
    return (values, targets)


def draw_samples(key, part):
    return joint_values(key)[0]


def draw_treatment_features(key, part):
    return joint_values(key)[1].astype(jnp.bfloat16)


def plant(array, stream_key, least, top_value):
    longest = array.shape.index(max(array.shape))
    spots = []
    for shift in (0, 1):
        where = [jax.random.randint(jax.random.fold_in(stream_key, axis), (), 0, length) for axis, length in enumerate(array.shape)]
        where[longest] = (where[longest] + shift) % array.shape[longest]
        spots.append(tuple(where))
    return array.at[spots[0]].set(least).at[spots[1]].set(top_value)


def gaussian(rng, extent, deviation, reach, kind=jnp.bfloat16):
    entries = deviation * jax.random.normal(rng, extent, jnp.float32)
    return jnp.clip(entries, min=-reach, max=reach).astype(kind)


def setup_inputs(seed: int = 0) -> dict:
    streams_of = jax.random.split(jax.random.key(seed), 6)
    return {
        "samples": draw_samples(jax.random.fold_in(streams_of[5], 71), 0),
        "freq_table": gaussian(streams_of[1], (NFREQ, DX), 0.5, 3.0, jnp.float32),
        "feature_seeds": plant(jax.random.randint(streams_of[2], (M,), 0, NFREQ), jax.random.fold_in(streams_of[2], 1), 0, NFREQ - 1).astype(jnp.int32),
        "phases": jnp.clip(jax.random.uniform(streams_of[3], (M,), jnp.float32, -3.140625, 3.140625), -3.140625, 3.140625),
        "treatment_features": draw_treatment_features(jax.random.fold_in(streams_of[5], 71), 0),
    }


ridge = 0.05

def solve_with(factor, right):
    lower = lax.linalg.triangular_solve(factor, right, left_side=True, lower=True)
    return lax.linalg.triangular_solve(factor, lower, left_side=True, lower=True, transpose_a=True)

def reference(samples, freq_table, feature_seeds, phases, treatment_features):
    count = samples.shape[0]
    freqs = freq_table[feature_seeds.astype(jnp.int32)]
    angles = jnp.dot(samples.astype(jnp.float32), freqs.T.astype(jnp.float32), precision=lax.Precision.HIGHEST, preferred_element_type=jnp.float32) + phases
    instruments = (jnp.sqrt(jnp.float32(2.0)) * jnp.cos(angles)).astype(jnp.bfloat16)
    gram = jnp.dot(instruments.T.astype(jnp.float32), instruments.astype(jnp.float32), preferred_element_type=jnp.float32) / count
    gram = gram + ridge * jnp.eye(gram.shape[0], dtype=jnp.float32)
    cross = jnp.dot(instruments.T.astype(jnp.float32), treatment_features.astype(jnp.float32), preferred_element_type=jnp.float32) / count
    factor = jnp.linalg.cholesky(gram)
    coefficients = solve_with(factor, cross)
    fitted = jnp.dot(instruments.astype(jnp.float32), coefficients.astype(jnp.bfloat16).astype(jnp.float32), preferred_element_type=jnp.float32)
    return (coefficients, fitted)
```

```python
import math

import jax
import jax.numpy as jnp
import numpy as np
from jax import lax
from jax.experimental import pallas as pl
from jax.experimental.pallas import tpu as pltpu
from jax.sharding import Mesh
from jax.sharding import PartitionSpec as P

ROWS = ("y", "x", "c")
ALL = ("y", "x", "c", "z")
RIDGE = 0.05
M = 512
TILE = 128
F32, BF16 = jnp.float32, jnp.bfloat16
MIB = 1 << 20


def sine_coefficients():
    nodes = 0.25 * np.cos(np.pi * (np.arange(400) + 0.5) / 800)
    powers = np.stack([nodes ** (2 * k + 1) for k in range(5)], 1)
    return [float(c) for c in np.linalg.lstsq(powers, np.sqrt(2) * np.sin(2 * np.pi * nodes), rcond=None)[0]]


COEFFS = sine_coefficients()


def split3(a):
    hi = a.astype(BF16)
    rest = a - hi.astype(F32)
    mid = rest.astype(BF16)
    low = (rest - mid.astype(F32)).astype(BF16)
    return hi, mid, low


def split2(a):
    hi = a.astype(BF16)
    return hi, (a - hi.astype(F32)).astype(BF16)


def dot(a, b, ca=1, cb=0):
    return lax.dot_general(a, b, (((ca,), (cb,)), ((), ())), preferred_element_type=F32)


def dot_pieces(a, b, cb=0):
    total = None
    n = len(a)
    for i in reversed(range(n)):
        for j in reversed(range(n - i)):
            term = dot(a[i], b[j], 1, cb)
            total = term if total is None else total + term
    return total


def select_frequencies(table_ref, seeds_ref, phases_ref):
    seeds = seeds_ref[...]
    near = jnp.bitwise_and(seeds, TILE - 1)
    far = jnp.right_shift(seeds, 7)
    hot = jnp.where(lax.broadcasted_iota(jnp.int32, (TILE, M), 0) == near, 1.0, 0.0).astype(BF16)
    groups = table_ref.shape[1] // TILE
    table = jnp.concatenate([table_ref[:, g * TILE : (g + 1) * TILE] for g in range(groups)], 0)
    pieces = split3(table)
    rows = (dot(pieces[0], hot) + dot(pieces[1], hot)) + dot(pieces[2], hot)
    freqs = jnp.zeros((16, M), F32)
    for g in range(groups):
        freqs = freqs + jnp.where(far == g, rows[g * 16 : (g + 1) * 16], 0.0)
    turns = F32(1 / (2 * math.pi))
    f1, f2, f3 = split3(freqs * turns)
    p1, p2, p3 = (jnp.broadcast_to(p.astype(F32), (16, M)) for p in split3(phases_ref[...] * turns))
    line = lax.broadcasted_iota(jnp.int32, (16, M), 0)
    offset = jnp.where(line == 0, p1, jnp.where(line == 1, p2, jnp.where(line == 2, p3, 0.0))).astype(BF16)
    return jnp.concatenate([f1, f2, f3, f1, f2, f1, offset], 0)


def features(x, freqs):
    x1, x2, x3 = split3(x)
    ones = jnp.ones((16, x.shape[1]), BF16)
    angle = dot(jnp.concatenate([x1, x1, x1, x2, x2, x3, ones], 0), freqs, 0, 0)
    angle = angle - jnp.round(angle)
    q = 0.25 - jnp.abs(angle)
    s = q * q
    p = COEFFS[4] * s + COEFFS[3]
    for c in COEFFS[2::-1]:
        p = p * s + c
    return (p * q).astype(BF16)


CHUNK = 256


def own_kernel(place_ref, table_ref, seeds_ref, phases_ref, x_ref, t_ref, freqs_ref, z_ref, gram_ref, cross_ref):
    freqs = select_frequencies(table_ref, seeds_ref, phases_ref)
    freqs_ref[...] = freqs
    cross = jnp.zeros(cross_ref.shape, F32)
    for k in range(0, x_ref.shape[1], CHUNK):
        z = features(x_ref[:, k : k + CHUNK], freqs)
        z_ref[k : k + CHUNK, :] = z
        cross = cross + dot(t_ref[:, k : k + CHUNK], z)
    cross_ref[...] = cross
    at = 0
    for i in range(M // TILE):
        width = (i + 1) * TILE
        block = dot(z_ref[:, i * TILE : width], z_ref[:, :width], 0, 0)
        for j in range(i + 1):
            gram_ref[at : at + TILE, :] = block[:, j * TILE : (j + 1) * TILE]
            at += TILE


def more_kernel(blocks, tiled, place_ref, freqs_ref, before_ref, *refs):
    xs, ts, out_ref = refs[:blocks], refs[blocks : 2 * blocks], refs[2 * blocks]
    freqs = freqs_ref[...]
    cross = before_ref[...]
    for x_ref, t_ref in zip(xs, ts):
        for k in range(0, x_ref.shape[1], CHUNK):
            z = features(x_ref[:, k : k + CHUNK], freqs)
            cross = cross + dot(t_ref[:, k : k + CHUNK], z)
    if tiled:
        across = M // TILE
        for r in range(out_ref.shape[0]):
            i, j = divmod(r, across)
            out_ref[r] = cross[8 * i : 8 * i + 8, TILE * j : TILE * (j + 1)]
    else:
        out_ref[...] = cross


def inverse_kernel(packed_ref, gram_ref, inverse_ref, *, scale):
    at = 0
    for i in range(M // TILE):
        for j in range(i + 1):
            block = packed_ref[at : at + TILE, :] * scale
            if i == j:
                line = lax.broadcasted_iota(jnp.int32, (TILE, TILE), 0)
                lane = lax.broadcasted_iota(jnp.int32, (TILE, TILE), 1)
                block = block + jnp.where(line == lane, F32(RIDGE), 0.0)
            gram_ref[i * TILE : (i + 1) * TILE, j * TILE : (j + 1) * TILE] = block
            if i != j:
                gram_ref[j * TILE : (j + 1) * TILE, i * TILE : (i + 1) * TILE] = block.T
            at += TILE
    gram = gram_ref[...]
    line = lax.broadcasted_iota(jnp.int32, (M, M), 0)
    lane = lax.broadcasted_iota(jnp.int32, (M, M), 1)
    twice = jnp.where(line == lane, F32(2), F32(0))
    sums = jnp.sum(jnp.abs(gram), axis=0, keepdims=True)
    top = jnp.max(sums, axis=1, keepdims=True)
    low = jnp.full((1, 1), RIDGE * 0.999, F32)
    first = 2.0 / (top + low)
    error = (top - low) / (top + low)
    gain = 2.0 / (2.0 - error * error)
    inverse_ref[...] = (gain * first) * (twice - first * gram)
    error = error * error * 0.5 * gain
    g = split2(gram)

    def more(state):
        return jnp.max(state) > 2e-3

    def step(error):
        gain = 2.0 / (2.0 - error * error)
        x = inverse_ref[...]
        pieces = split2(x)
        rest = twice - dot_pieces(g, pieces)
        inverse_ref[...] = gain * dot_pieces(pieces, split2(rest))
        return error * error * 0.5 * gain

    lax.while_loop(more, step, error)


def coefficients_kernel(gram_ref, inverse_ref, tiles_ref, out_ref, cross_ref, *, scale):
    across = M // TILE
    for r in range(tiles_ref.shape[0]):
        i, j = divmod(r, across)
        for z in range(tiles_ref.shape[1]):
            first = z * (M // tiles_ref.shape[1]) + 8 * i
            cross_ref[first : first + 8, TILE * j : TILE * (j + 1)] = tiles_ref[r, z] * scale
    cross = cross_ref[...].T
    x = split2(inverse_ref[...])
    guess = dot_pieces(x, split2(cross))
    rest = cross - dot_pieces(split3(gram_ref[...]), split3(guess))
    out_ref[...] = guess + dot_pieces(x, split2(rest))


def fitted_kernel(z_ref, coef_ref, out_ref):
    out_ref[...] = dot(z_ref[...], coef_ref[...].astype(BF16))


def params(mib=48):
    return pltpu.CompilerParams(vmem_limit_bytes=mib * MIB)


def full(shape):
    return pl.BlockSpec(shape, lambda *_: (0,) * len(shape))


def shaped(shape, dtype=F32):
    return jax.ShapeDtypeStruct(shape, dtype)


def own_part(place, table, seeds, phases, x, t):
    own, cols = x.shape[1], t.shape[0]
    return pl.pallas_call(
        own_kernel,
        grid_spec=pltpu.PrefetchScalarGridSpec(
            num_scalar_prefetch=1,
            grid=(1,),
            in_specs=[
                full(table.shape),
                full(seeds.shape),
                full(phases.shape),
                full(x.shape),
                pl.BlockSpec((cols, own), lambda _, place: (0, place[0])),
            ],
            out_specs=[full((112, M)), full((own, M)), full((1280, TILE)), full((cols, M))],
        ),
        out_shape=[shaped((112, M), BF16), shaped((own, M), BF16), shaped((1280, TILE)), shaped((cols, M))],
        compiler_params=params(),
        name="own_part",
    )(place, table, seeds, phases, x, t)


def more_cross(place, freqs, before, xs, t, tiled):
    own, cols = xs[0].shape[1], t.shape[0]
    n = len(xs)
    out = (cols * M // (8 * TILE), 8, TILE) if tiled else (cols, M)

    def kernel(*refs):
        more_kernel(n, tiled, *refs)

    return pl.pallas_call(
        kernel,
        grid_spec=pltpu.PrefetchScalarGridSpec(
            num_scalar_prefetch=1,
            grid=(1,),
            in_specs=[full(freqs.shape), full(before.shape)]
            + [full(x.shape) for x in xs]
            + [pl.BlockSpec((cols, own), lambda _, place, k=k: (0, place[k])) for k in range(n)],
            out_specs=full(out),
        ),
        out_shape=shaped(out),
        compiler_params=params(),
        name="more_cross",
    )(place, freqs, before, *xs, *([t] * n))


def whole_vmem():
    return pl.BlockSpec(memory_space=pltpu.VMEM)


def inverted(packed, count):
    def kernel(*refs):
        inverse_kernel(*refs, scale=1.0 / count)

    return pl.pallas_call(
        kernel,
        in_specs=[whole_vmem()],
        out_specs=[whole_vmem()] * 2,
        out_shape=[shaped((M, M))] * 2,
        compiler_params=params(),
        name="inverted",
    )(packed)


def solved(gram, inverse, tiles, count):
    def kernel(*refs):
        coefficients_kernel(*refs, scale=1.0 / count)

    return pl.pallas_call(
        kernel,
        in_specs=[whole_vmem()] * 3,
        out_specs=whole_vmem(),
        out_shape=shaped((M, M)),
        scratch_shapes=[pltpu.VMEM((M, M), F32)],
        compiler_params=params(),
        name="solved",
    )(gram, inverse, tiles)


def predicted(z, coef):
    own = z.shape[0]
    lines = 512
    return pl.pallas_call(
        fitted_kernel,
        grid=(own // lines,),
        in_specs=[pl.BlockSpec((lines, M), lambda i: (i, 0)), full((M, M))],
        out_specs=pl.BlockSpec((lines, M), lambda i: (i, 0)),
        out_shape=shaped((own, M)),
        compiler_params=params(),
        name="predicted",
    )(z, coef)


def to_all(array, axes):
    n = lax.axis_size(axes)
    return lax.all_to_all(jnp.broadcast_to(array[None], (n, *array.shape)), axes, 0, 0, tiled=True)


def scattered_sum(array, axes):
    return lax.all_to_all(array, axes, 0, 0, tiled=True).sum(axis=0)


def body(samples, freq_table, feature_seeds, phases, treatment_features):
    count = samples.shape[0] * lax.axis_size(ROWS) * lax.axis_size("z")
    turn = lax.axis_size("z")
    rows = lax.axis_size(ROWS)
    here = lax.axis_index("z").astype(jnp.int32)
    x = samples.T
    t = treatment_features.T

    def place(*shifts):
        return jnp.stack([lax.rem(here + (s % turn), turn) for s in shifts])

    ahead = [(k, (k + 1) % turn) for k in range(turn)]
    back = [(k, (k - 1) % turn) for k in range(turn)]
    right, left = [x], [x]
    for _ in range(turn // 2):
        right.append(lax.ppermute(right[-1], "z", ahead))
    for _ in range(turn // 2 - 1):
        left.append(lax.ppermute(left[-1], "z", back))

    freqs, z, gram_part, cross = own_part(
        place(0), freq_table.T, feature_seeds[None, :], phases[None, :], x, t
    )
    gram = scattered_sum(gram_part.reshape(rows, -1, TILE), ROWS)
    gram = to_all(gram, "z").sum(axis=0)
    gram = to_all(gram, ROWS).reshape(-1, TILE)
    for k in range(1, turn // 2 - 1):
        cross = more_cross(place(-k, k), freqs, cross, [right[k], left[k]], t, False)
    k = turn // 2 - 1
    cross = more_cross(place(-k, k, -k - 1), freqs, cross, [right[k], left[k], right[k + 1]], t, True)
    cross = scattered_sum(cross, ROWS)
    cross = to_all(to_all(cross, "z"), ROWS)
    gram, inverse = inverted(gram, count)
    coefficients = solved(gram, inverse, cross, count)
    return coefficients, predicted(z, coefficients)


def solution(mesh):
    turn = mesh.shape["rhs"]
    torus = Mesh(mesh.devices.reshape(4, 4, 2, turn), ALL)
    placed = (P(ALL, None), P(), P(), P(), P(ROWS, "z"))
    return jax.shard_map(body, mesh=torus, in_specs=placed, out_specs=(P(), P(ALL, None)), check_vma=False)
```

```python
import math

import jax
import jax.numpy as jnp
import numpy as np
from jax import lax
from jax.experimental import pallas as pl
from jax.experimental.pallas import tpu as pltpu
from jax.sharding import Mesh
from jax.sharding import PartitionSpec as P

ROWS = ("y", "x", "c")
ALL = ("y", "x", "c", "z")
RIDGE = 0.05
M = 512
TILE = 128
F32, BF16 = jnp.float32, jnp.bfloat16
MIB = 1 << 20


def sine_coefficients():
    nodes = 0.25 * np.cos(np.pi * (np.arange(400) + 0.5) / 800)
    powers = np.stack([nodes ** (2 * k + 1) for k in range(5)], 1)
    return [float(c) for c in np.linalg.lstsq(powers, np.sqrt(2) * np.sin(2 * np.pi * nodes), rcond=None)[0]]


COEFFS = sine_coefficients()


def split3(a):
    hi = a.astype(BF16)
    rest = a - hi.astype(F32)
    mid = rest.astype(BF16)
    low = (rest - mid.astype(F32)).astype(BF16)
    return hi, mid, low


def split2(a):
    hi = a.astype(BF16)
    return hi, (a - hi.astype(F32)).astype(BF16)


def dot(a, b, ca=1, cb=0):
    return lax.dot_general(a, b, (((ca,), (cb,)), ((), ())), preferred_element_type=F32)


def dot_pieces(a, b, cb=0):
    total = None
    n = len(a)
    for i in reversed(range(n)):
        for j in reversed(range(n - i)):
            term = dot(a[i], b[j], 1, cb)
            total = term if total is None else total + term
    return total


def select_frequencies(table_ref, seeds_ref, phases_ref):
    seeds = seeds_ref[...]
    near = jnp.bitwise_and(seeds, TILE - 1)
    far = jnp.right_shift(seeds, 7)
    hot = jnp.where(lax.broadcasted_iota(jnp.int32, (TILE, M), 0) == near, 1.0, 0.0).astype(BF16)
    groups = table_ref.shape[1] // TILE
    table = jnp.concatenate([table_ref[:, g * TILE : (g + 1) * TILE] for g in range(groups)], 0)
    pieces = split3(table)
    rows = (dot(pieces[0], hot) + dot(pieces[1], hot)) + dot(pieces[2], hot)
    freqs = jnp.zeros((16, M), F32)
    for g in range(groups):
        freqs = freqs + jnp.where(far == g, rows[g * 16 : (g + 1) * 16], 0.0)
    turns = F32(1 / (2 * math.pi))
    f1, f2, f3 = split3(freqs * turns)
    p1, p2, p3 = (jnp.broadcast_to(p.astype(F32), (16, M)) for p in split3(phases_ref[...] * turns))
    line = lax.broadcasted_iota(jnp.int32, (16, M), 0)
    offset = jnp.where(line == 0, p1, jnp.where(line == 1, p2, jnp.where(line == 2, p3, 0.0))).astype(BF16)
    return jnp.concatenate([f1, f2, f3, f1, f2, f1, offset], 0)


def stacked(x):
    x1, x2, x3 = split3(x)
    return jnp.concatenate([x1, x1, x1, x2, x2, x3, jnp.ones((16, x.shape[1]), BF16)], 0)


def cosines(angle):
    angle = angle - jnp.round(angle)
    q = 0.25 - jnp.abs(angle)
    s = q * q
    p = COEFFS[4] * s + COEFFS[3]
    for c in COEFFS[2::-1]:
        p = p * s + c
    return (p * q).astype(BF16)


CHUNK = 512


def copied(pairs, sems):
    copies = [pltpu.make_async_copy(src, dst, sems.at[k]) for k, (src, dst) in enumerate(pairs)]
    for copy in copies:
        copy.start()
    return copies


def add_block(x, freqs, panel, lhs, z):
    for c in range(0, z.shape[0], CHUNK):
        span = slice(c, c + CHUNK)
        pieces = stacked(x[:, span])
        z[span, :] = cosines(dot(pieces, freqs, 0, 0))
        lhs[lhs.shape[0] - panel.shape[0] :, span] = cosines(dot(panel, pieces))


def block_of(t_hbm, shift, turn, own):
    at = pl.multiple_of(lax.rem(lax.axis_index("z") + shift % turn, turn) * own, own)
    return t_hbm.at[:, pl.ds(at, own)]


def own_kernel(turn, table_hbm, seeds_hbm, phases_hbm, x_hbm, t_hbm, *refs):
    freqs_ref, panel_ref, total_ref, z_hbm, table, seeds, phases, x, z, lhs, sems = refs
    own, cols = z.shape[0], t_hbm.shape[0]
    pairs = [(table_hbm, table), (seeds_hbm, seeds), (phases_hbm, phases), (x_hbm, x)]
    pairs.append((block_of(t_hbm, 0, turn, own), lhs.at[:cols]))
    copies = copied(pairs, sems)
    for copy in copies[:4]:
        copy.wait()
    freqs = select_frequencies(table, seeds, phases)
    freqs_ref[...] = freqs
    wide = panel_ref.shape[0]
    line = lax.broadcasted_iota(jnp.int32, (wide, M), 0) + wide * lax.axis_index("z")
    chosen = jnp.where(line == lax.broadcasted_iota(jnp.int32, (wide, M), 1), 1.0, 0.0).astype(BF16)
    panel = dot(chosen, freqs, 1, 1).astype(BF16)
    panel_ref[...] = panel
    add_block(x, freqs, panel, lhs, z)
    out = pltpu.make_async_copy(z, z_hbm, sems.at[5])
    out.start()
    copies[4].wait()
    total_ref[...] = dot(lhs[...], z[...])
    out.wait()


def more_kernel(shifts, tiled, turn, freqs_ref, panel_ref, before_ref, t_hbm, *refs):
    n = len(shifts)
    xs, (out_ref, lhs, z, sems) = refs[:n], refs[n:]
    own, cols = z.shape[0], t_hbm.shape[0]
    copies = copied([(block_of(t_hbm, s, turn, own), lhs.at[k, :cols]) for k, s in enumerate(shifts)], sems)
    freqs, panel = freqs_ref[...], panel_ref[...]
    total = before_ref[...]
    for k, x_ref in enumerate(xs):
        add_block(x_ref, freqs, panel, lhs.at[k], z)
        copies[k].wait()
        total = total + dot(lhs[k], z[...])
    if tiled:
        across = M // TILE
        for r in range(out_ref.shape[0]):
            i, j = divmod(r, across)
            lanes = slice(TILE * j, TILE * (j + 1))
            out_ref[r, :8] = total[cols + 8 * i : cols + 8 * i + 8, lanes]
            out_ref[r, 8:] = total[8 * i : 8 * i + 8, lanes]
    else:
        out_ref[...] = total


PANELS = 6


def panel_of(block, k):
    return 2 * ((block + k // 2) % (M // TILE)) + k % 2


def pack_kernel(parts_ref, gram_ref, cross_ref):
    column = (2 * lax.axis_index("x") + lax.axis_index("c")) % (M // TILE)
    for k in range(PANELS):
        tile = parts_ref[panel_of(column, k)][:8]
        for r in range(gram_ref.shape[0]):
            gram_ref[r, k] = tile
    for z in range(parts_ref.shape[0]):
        tile = parts_ref[z, 8:]
        for r in range(cross_ref.shape[0]):
            cross_ref[r, z] = tile


def spread_kernel(parts, out_ref):
    total = parts[0]
    for k in range(1, parts.shape[0]):
        total = total + parts[k]
    for k in range(out_ref.shape[0]):
        out_ref[k] = total


def inverse_kernel(scale, packed_ref, inverse_ref, gram_ref):
    across = M // TILE
    for r in range(packed_ref.shape[0]):
        i, j = divmod(r, across)
        for k in range(PANELS):
            first = 64 * panel_of(j, k) + 8 * i
            gram_ref[first : first + 8, TILE * j : TILE * (j + 1)] = packed_ref[r, k] * scale
    for i in range(across):
        j = (i + 1) % across
        lower = slice(TILE * i, TILE * (i + 1)), slice(TILE * j, TILE * (j + 1))
        gram_ref[lower] = gram_ref[lower[::-1]].T
    line = lax.broadcasted_iota(jnp.int32, (M, M), 0)
    lane = lax.broadcasted_iota(jnp.int32, (M, M), 1)
    twice = jnp.where(line == lane, F32(2), F32(0))
    gram = gram_ref[...] + (RIDGE / 2) * twice
    gram_ref[...] = gram
    sums = jnp.sum(jnp.abs(gram), axis=0, keepdims=True)
    top = jnp.max(sums, axis=1, keepdims=True)
    low = jnp.full((1, 1), RIDGE * 0.999, F32)
    first = 2.0 / (top + low)
    error = (top - low) / (top + low)
    gain = 2.0 / (2.0 - error * error)
    inverse_ref[...] = (gain * first) * (twice - first * gram)
    error = error * error * 0.5 * gain
    g = split2(gram)

    def more(state):
        return jnp.max(state) > 2e-3

    def step(error):
        gain = 2.0 / (2.0 - error * error)
        x = inverse_ref[...]
        pieces = split2(x)
        rest = twice - dot_pieces(g, pieces)
        inverse_ref[...] = gain * dot_pieces(pieces, split2(rest))
        return error * error * 0.5 * gain

    lax.while_loop(more, step, error)
    x = inverse_ref[...]
    rest = twice - dot_pieces(split3(gram_ref[...]), split3(x))
    inverse_ref[...] = dot_pieces(split2(x), split2(rest))


def finish_kernel(scale, inverse_ref, tiles, z_hbm, coef_ref, fitted_hbm, cross_ref, z, fitted, sems):
    n = z.shape[0]
    lines = z.shape[1]
    spans = [pl.ds(k * lines, lines) for k in range(n)]
    copies = copied([(z_hbm.at[span], z.at[k]) for k, span in enumerate(spans)], sems)
    x = split2(inverse_ref[...])
    across = M // TILE
    for r in range(tiles.shape[0]):
        i, j = divmod(r, across)
        for k in range(tiles.shape[1]):
            first = k * (M // tiles.shape[1]) + 8 * i
            cross_ref[first : first + 8, TILE * j : TILE * (j + 1)] = tiles[r, k] * scale
    coef = dot_pieces(x, split2(cross_ref[...]), 1)
    coef_ref[...] = coef
    low = coef.astype(BF16)
    outs = []
    for k, span in enumerate(spans):
        copies[k].wait()
        fitted[k] = dot(z[k], low)
        out = pltpu.make_async_copy(fitted.at[k], fitted_hbm.at[span], sems.at[n + k])
        out.start()
        outs.append(out)
    for out in outs:
        out.wait()


def cost(us):
    return pl.CostEstimate(flops=int(us * 1.15e9), transcendentals=0, bytes_accessed=0)


def params(mib=48):
    return pltpu.CompilerParams(vmem_limit_bytes=mib * MIB)


def full(shape):
    return pl.BlockSpec(shape, lambda *_: (0,) * len(shape))


def shaped(shape, dtype=F32):
    return jax.ShapeDtypeStruct(shape, dtype)


HBM = pl.BlockSpec(memory_space=pltpu.HBM)
VMEM = pl.BlockSpec(memory_space=pltpu.VMEM)


def in_hbm(array):
    return pltpu.with_memory_space_constraint(array, pltpu.HBM)


def own_part(table, seeds, phases, x, t, turn):
    own, cols = x.shape[1], t.shape[0]
    wide = M // turn
    ins = (table, seeds, phases, x)

    def kernel(*refs):
        own_kernel(turn, *refs)

    return pl.pallas_call(
        kernel,
        in_specs=[HBM] * 5,
        out_specs=[VMEM, VMEM, VMEM, HBM],
        out_shape=[shaped((112, M), BF16), shaped((wide, 112), BF16), shaped((cols + wide, M)), shaped((own, M), BF16)],
        scratch_shapes=[pltpu.VMEM(a.shape, a.dtype) for a in ins]
        + [pltpu.VMEM((own, M), BF16), pltpu.VMEM((cols + wide, own), BF16), pltpu.SemaphoreType.DMA((6,))],
        compiler_params=params(),
        cost_estimate=cost(5),
        name="own_part",
    )(*(in_hbm(a) for a in ins), in_hbm(t))


def more_part(shifts, freqs, panel, before, xs, t, turn, tiled=False):
    own, cols = xs[0].shape[1], t.shape[0]
    n = len(xs)
    lines = before.shape[0]
    out = (cols * M // (8 * TILE), 8 * lines // cols, TILE) if tiled else before.shape

    def kernel(*refs):
        more_kernel(shifts, tiled, turn, *refs)

    return pl.pallas_call(
        kernel,
        in_specs=[VMEM, VMEM, VMEM, HBM] + [VMEM] * n,
        out_specs=VMEM,
        out_shape=shaped(out),
        scratch_shapes=[
            pltpu.VMEM((n, lines, own), BF16),
            pltpu.VMEM((own, M), BF16),
            pltpu.SemaphoreType.DMA((n,)),
        ],
        compiler_params=params(),
        cost_estimate=cost(2.6 * n),
        name="more_part",
    )(freqs, panel, before, in_hbm(t), *xs)


def spread(parts, copies):
    return pl.pallas_call(
        spread_kernel,
        in_specs=[VMEM],
        out_specs=VMEM,
        out_shape=shaped((copies, *parts.shape[1:])),
        compiler_params=params(),
        cost_estimate=cost(1),
        name="spread",
    )(parts)


def packed(parts, rows):
    return pl.pallas_call(
        pack_kernel,
        in_specs=[VMEM],
        out_specs=[VMEM, VMEM],
        out_shape=[shaped((rows, PANELS, 8, TILE)), shaped((rows, parts.shape[0], 8, TILE))],
        compiler_params=params(),
        cost_estimate=cost(1),
        name="packed",
    )(parts)


def inverted(tiles, count):
    def kernel(*refs):
        inverse_kernel(1.0 / count, *refs)

    return pl.pallas_call(
        kernel,
        in_specs=[VMEM],
        out_specs=VMEM,
        out_shape=shaped((M, M)),
        scratch_shapes=[pltpu.VMEM((M, M), F32)],
        compiler_params=params(),
        cost_estimate=cost(16),
        name="inverted",
    )(tiles)


def finished(inverse, tiles, z, count):
    own = z.shape[0]
    n = 4
    lines = own // n

    def kernel(*refs):
        finish_kernel(1.0 / count, *refs)

    return pl.pallas_call(
        kernel,
        in_specs=[VMEM, VMEM, HBM],
        out_specs=[VMEM, HBM],
        out_shape=[shaped((M, M)), shaped((own, M))],
        scratch_shapes=[
            pltpu.VMEM((M, M), F32),
            pltpu.VMEM((n, lines, M), BF16),
            pltpu.VMEM((n, lines, M), F32),
            pltpu.SemaphoreType.DMA((2 * n,)),
        ],
        compiler_params=params(),
        cost_estimate=cost(4),
        name="finished",
    )(inverse, tiles, z)


def exchanged(array, axes):
    return lax.all_to_all(array, axes, 0, 0, tiled=True)


def body(samples, freq_table, feature_seeds, phases, treatment_features):
    count = samples.shape[0] * lax.axis_size(ROWS) * lax.axis_size("z")
    turn = lax.axis_size("z")
    rows = lax.axis_size(ROWS)
    x = samples.T
    t = treatment_features.T

    ahead = [(k, (k + 1) % turn) for k in range(turn)]
    back = [(k, (k - 1) % turn) for k in range(turn)]
    right, left = [x], [x]
    half = turn // 2
    for _ in range(half):
        right.append(lax.ppermute(right[-1], "z", ahead))
    for _ in range(half - 1):
        left.append(lax.ppermute(left[-1], "z", back))

    freqs, panel, total, z = own_part(freq_table.T, feature_seeds[None, :], phases[None, :], x, t, turn)
    for k in range(1, half):
        total = more_part((-k, k), freqs, panel, total, (right[k], left[k]), t, turn)
    total = more_part((-half,), freqs, panel, total, (right[half],), t, turn, tiled=True)
    parts = exchanged(spread(exchanged(total, ROWS), turn), "z")
    gram, cross = packed(parts, rows)
    inverse = inverted(exchanged(gram, ROWS), count)
    cross = exchanged(cross, ROWS)
    return finished(inverse, cross, z, count)


def solution(mesh):
    turn = mesh.shape["rhs"]
    torus = Mesh(mesh.devices.reshape(4, 4, 2, turn), ALL)
    placed = (P(ALL, None), P(), P(), P(), P(ROWS, "z"))
    return jax.shard_map(body, mesh=torus, in_specs=placed, out_specs=(P(), P(ALL, None)), check_vma=False)
```

```python
import math

import jax
import jax.numpy as jnp
import numpy as np
from jax import lax
from jax.experimental import pallas as pl
from jax.experimental.pallas import tpu as pltpu
from jax.sharding import Mesh
from jax.sharding import PartitionSpec as P

ROWS = ("y", "x", "c")
ALL = ("y", "x", "c", "z")
RIDGE = 0.05
M = 512
TILE = 128
F32, BF16 = jnp.float32, jnp.bfloat16
MIB = 1 << 20


def sine_coefficients():
    nodes = 0.25 * np.cos(np.pi * (np.arange(400) + 0.5) / 800)
    powers = np.stack([nodes ** (2 * k + 1) for k in range(5)], 1)
    return [float(c) for c in np.linalg.lstsq(powers, np.sqrt(2) * np.sin(2 * np.pi * nodes), rcond=None)[0]]


COEFFS = sine_coefficients()


def split3(a):
    hi = a.astype(BF16)
    rest = a - hi.astype(F32)
    mid = rest.astype(BF16)
    low = (rest - mid.astype(F32)).astype(BF16)
    return hi, mid, low


def split2(a):
    hi = a.astype(BF16)
    return hi, (a - hi.astype(F32)).astype(BF16)


def dot(a, b, ca=1, cb=0):
    return lax.dot_general(a, b, (((ca,), (cb,)), ((), ())), preferred_element_type=F32)


def dot_pieces(a, b, cb=0):
    n = len(a)
    pairs = [(i, j) for i in reversed(range(n)) for j in reversed(range(n - i))]
    return dot(
        jnp.concatenate([a[i] for i, _ in pairs], 1),
        jnp.concatenate([b[j] for _, j in pairs], cb),
        1,
        cb,
    )


def select_frequencies(table_ref, seeds_ref, phases_ref):
    seeds = seeds_ref[...]
    near = jnp.bitwise_and(seeds, TILE - 1)
    far = jnp.right_shift(seeds, 7)
    hot = jnp.where(lax.broadcasted_iota(jnp.int32, (TILE, M), 0) == near, 1.0, 0.0).astype(BF16)
    groups = table_ref.shape[1] // TILE
    table = jnp.concatenate([table_ref[:, g * TILE : (g + 1) * TILE] for g in range(groups)], 0)
    pieces = split3(table)
    rows = (dot(pieces[0], hot) + dot(pieces[1], hot)) + dot(pieces[2], hot)
    freqs = jnp.zeros((16, M), F32)
    for g in range(groups):
        freqs = freqs + jnp.where(far == g, rows[g * 16 : (g + 1) * 16], 0.0)
    turns = F32(1 / (2 * math.pi))
    f1, f2, f3 = split3(freqs * turns)
    p1, p2, p3 = (jnp.broadcast_to(p.astype(F32), (16, M)) for p in split3(phases_ref[...] * turns))
    line = lax.broadcasted_iota(jnp.int32, (16, M), 0)
    offset = jnp.where(line == 0, p1, jnp.where(line == 1, p2, jnp.where(line == 2, p3, 0.0))).astype(BF16)
    return jnp.concatenate([f1, f2, f3, f1, f2, f1, offset], 0)


def stacked(x):
    x1, x2, x3 = split3(x)
    return jnp.concatenate([x1, x1, x1, x2, x2, x3, jnp.ones((16, x.shape[1]), BF16)], 0)


def cosines(angle):
    angle = angle - jnp.round(angle)
    q = 0.25 - jnp.abs(angle)
    s = q * q
    p = COEFFS[4] * s + COEFFS[3]
    for c in COEFFS[2::-1]:
        p = p * s + c
    return (p * q).astype(BF16)


CHUNK = 512


def copied(pairs, sems):
    copies = [pltpu.make_async_copy(src, dst, sems.at[k]) for k, (src, dst) in enumerate(pairs)]
    for copy in copies:
        copy.start()
    return copies


def add_block(x, freqs, panel, lhs, z):
    for c in range(0, z.shape[0], CHUNK):
        span = slice(c, c + CHUNK)
        pieces = stacked(x[:, span])
        z[span, :] = cosines(dot(pieces, freqs, 0, 0))
        lhs[lhs.shape[0] - panel.shape[0] :, span] = cosines(dot(panel, pieces))


def block_of(t_hbm, shift, turn, own):
    at = pl.multiple_of(lax.rem(lax.axis_index("z") + shift % turn, turn) * own, own)
    return t_hbm.at[:, pl.ds(at, own)]


def own_kernel(turn, table_hbm, seeds_hbm, phases_hbm, x_hbm, t_hbm, *refs):
    freqs_ref, panel_ref, total_ref, z_hbm, table, seeds, phases, x, z, lhs, sems = refs
    own, cols = z.shape[0], t_hbm.shape[0]
    pairs = [(table_hbm, table), (seeds_hbm, seeds), (phases_hbm, phases), (x_hbm, x)]
    pairs.append((block_of(t_hbm, 0, turn, own), lhs.at[:cols]))
    copies = copied(pairs, sems)
    for copy in copies[:4]:
        copy.wait()
    freqs = select_frequencies(table, seeds, phases)
    freqs_ref[...] = freqs
    wide = panel_ref.shape[0]
    line = lax.broadcasted_iota(jnp.int32, (wide, M), 0) + wide * lax.axis_index("z")
    chosen = jnp.where(line == lax.broadcasted_iota(jnp.int32, (wide, M), 1), 1.0, 0.0).astype(BF16)
    panel = dot(chosen, freqs, 1, 1).astype(BF16)
    panel_ref[...] = panel
    add_block(x, freqs, panel, lhs, z)
    out = pltpu.make_async_copy(z, z_hbm, sems.at[5])
    out.start()
    copies[4].wait()
    total_ref[...] = dot(lhs[...], z[...])
    out.wait()


def more_kernel(shifts, tiled, turn, freqs_ref, panel_ref, before_ref, t_hbm, *refs):
    n = len(shifts)
    xs, (out_ref, lhs, z, sems) = refs[:n], refs[n:]
    own, cols = z.shape[0], t_hbm.shape[0]
    copies = copied([(block_of(t_hbm, s, turn, own), lhs.at[k, :cols]) for k, s in enumerate(shifts)], sems)
    freqs, panel = freqs_ref[...], panel_ref[...]
    total = before_ref[...]
    for k, x_ref in enumerate(xs):
        add_block(x_ref, freqs, panel, lhs.at[k], z)
        copies[k].wait()
        total = total + dot(lhs[k], z[...])
    if tiled:
        across = M // TILE
        for r in range(out_ref.shape[0]):
            i, j = divmod(r, across)
            lanes = slice(TILE * j, TILE * (j + 1))
            out_ref[r, :8] = total[cols + 8 * i : cols + 8 * i + 8, lanes]
            out_ref[r, 8:] = total[8 * i : 8 * i + 8, lanes]
    else:
        out_ref[...] = total


PANELS = 6


def panel_of(block, k):
    return 2 * ((block + k // 2) % (M // TILE)) + k % 2


def pack_kernel(parts_ref, gram_ref, cross_ref):
    column = (2 * lax.axis_index("x") + lax.axis_index("c")) % (M // TILE)
    for k in range(PANELS):
        tile = parts_ref[panel_of(column, k)][:8]
        for r in range(gram_ref.shape[0]):
            gram_ref[r, k] = tile
    for z in range(parts_ref.shape[0]):
        tile = parts_ref[z, 8:]
        for r in range(cross_ref.shape[0]):
            cross_ref[r, z] = tile


def spread_kernel(parts, out_ref):
    total = parts[0]
    for k in range(1, parts.shape[0]):
        total = total + parts[k]
    for k in range(out_ref.shape[0]):
        out_ref[k] = total


def inverse_kernel(scale, mine_ref, other_ref, inverse_ref, gram_ref):
    across = M // TILE
    core = lax.axis_index("c")
    for r in range(2 * mine_ref.shape[0]):
        i, j = divmod(r, across)
        for k in range(PANELS):
            first = 64 * panel_of(j, k) + 8 * i
            tile = jnp.where(core == r % 2, mine_ref[r // 2, k], other_ref[r // 2, k])
            gram_ref[first : first + 8, TILE * j : TILE * (j + 1)] = tile * scale
    for i in range(across):
        j = (i + 1) % across
        lower = slice(TILE * i, TILE * (i + 1)), slice(TILE * j, TILE * (j + 1))
        gram_ref[lower] = gram_ref[lower[::-1]].T
    line = lax.broadcasted_iota(jnp.int32, (M, M), 0)
    lane = lax.broadcasted_iota(jnp.int32, (M, M), 1)
    twice = jnp.where(line == lane, F32(2), F32(0))
    gram = gram_ref[...] + (RIDGE / 2) * twice
    gram_ref[...] = gram
    sums = jnp.sum(jnp.abs(gram), axis=0, keepdims=True)
    top = jnp.max(sums, axis=1, keepdims=True)
    low = jnp.full((1, 1), RIDGE * 0.999, F32)
    first = 2.0 / (top + low)
    error = (top - low) / (top + low)
    gain = 2.0 / (2.0 - error * error)
    inverse_ref[...] = (gain * first) * (twice - first * gram)
    error = error * error * 0.5 * gain
    g = split2(gram)

    def more(state):
        return jnp.max(state) > 2e-3

    def step(error):
        gain = 2.0 / (2.0 - error * error)
        x = inverse_ref[...]
        pieces = split2(x)
        rest = twice - dot_pieces(g, pieces)
        inverse_ref[...] = gain * dot_pieces(pieces, split2(rest))
        return error * error * 0.5 * gain

    lax.while_loop(more, step, error)
    x = inverse_ref[...]
    rest = 0.5 * twice - dot_pieces(split3(gram_ref[...]), split3(x))
    inverse_ref[...] = x + dot(x.astype(BF16), rest.astype(BF16))


def finish_kernel(scale, inverse_ref, tiles, z_hbm, coef_ref, fitted_hbm, cross_ref, z, fitted, sems):
    n = z.shape[0]
    lines = z.shape[1]
    spans = [pl.ds(k * lines, lines) for k in range(n)]
    copies = copied([(z_hbm.at[span], z.at[k]) for k, span in enumerate(spans)], sems)
    x = split2(inverse_ref[...])
    across = M // TILE
    for r in range(tiles.shape[0]):
        i, j = divmod(r, across)
        for k in range(tiles.shape[1]):
            first = k * (M // tiles.shape[1]) + 8 * i
            cross_ref[first : first + 8, TILE * j : TILE * (j + 1)] = tiles[r, k] * scale
    coef = dot_pieces(x, split2(cross_ref[...]), 1)
    coef_ref[...] = coef
    low = coef.astype(BF16)
    outs = []
    for k, span in enumerate(spans):
        copies[k].wait()
        fitted[k] = dot(z[k], low)
        out = pltpu.make_async_copy(fitted.at[k], fitted_hbm.at[span], sems.at[n + k])
        out.start()
        outs.append(out)
    for out in outs:
        out.wait()


def cost(us):
    return pl.CostEstimate(flops=int(us * 1.15e9), transcendentals=0, bytes_accessed=0)


def params(mib=48):
    return pltpu.CompilerParams(vmem_limit_bytes=mib * MIB)


def full(shape):
    return pl.BlockSpec(shape, lambda *_: (0,) * len(shape))


def shaped(shape, dtype=F32):
    return jax.ShapeDtypeStruct(shape, dtype)


HBM = pl.BlockSpec(memory_space=pltpu.HBM)
VMEM = pl.BlockSpec(memory_space=pltpu.VMEM)


def in_hbm(array):
    return pltpu.with_memory_space_constraint(array, pltpu.HBM)


def own_part(table, seeds, phases, x, t, turn):
    own, cols = x.shape[1], t.shape[0]
    wide = M // turn
    ins = (table, seeds, phases, x)

    def kernel(*refs):
        own_kernel(turn, *refs)

    return pl.pallas_call(
        kernel,
        in_specs=[HBM] * 5,
        out_specs=[VMEM, VMEM, VMEM, HBM],
        out_shape=[shaped((112, M), BF16), shaped((wide, 112), BF16), shaped((cols + wide, M)), pltpu.HBM((own, M), BF16)],
        scratch_shapes=[pltpu.VMEM(a.shape, a.dtype) for a in ins]
        + [pltpu.VMEM((own, M), BF16), pltpu.VMEM((cols + wide, own), BF16), pltpu.SemaphoreType.DMA((6,))],
        compiler_params=params(),
        cost_estimate=cost(5),
        name="own_part",
    )(*(in_hbm(a) for a in ins), in_hbm(t))


def more_part(shifts, freqs, panel, before, xs, t, turn, tiled=False):
    own, cols = xs[0].shape[1], t.shape[0]
    n = len(xs)
    lines = before.shape[0]
    out = (cols * M // (8 * TILE), 8 * lines // cols, TILE) if tiled else before.shape

    def kernel(*refs):
        more_kernel(shifts, tiled, turn, *refs)

    return pl.pallas_call(
        kernel,
        in_specs=[VMEM, VMEM, VMEM, HBM] + [VMEM] * n,
        out_specs=VMEM,
        out_shape=shaped(out),
        scratch_shapes=[
            pltpu.VMEM((n, lines, own), BF16),
            pltpu.VMEM((own, M), BF16),
            pltpu.SemaphoreType.DMA((n,)),
        ],
        compiler_params=params(),
        cost_estimate=cost(2.6 * n),
        name="more_part",
    )(freqs, panel, before, in_hbm(t), *xs)


def spread(parts, copies):
    return pl.pallas_call(
        spread_kernel,
        in_specs=[VMEM],
        out_specs=VMEM,
        out_shape=shaped((copies, *parts.shape[1:])),
        compiler_params=params(),
        cost_estimate=cost(1),
        name="spread",
    )(parts)


def packed(parts, rows):
    return pl.pallas_call(
        pack_kernel,
        in_specs=[VMEM],
        out_specs=[VMEM, VMEM],
        out_shape=[shaped((rows // 2, PANELS, 8, TILE)), shaped((rows, parts.shape[0], 8, TILE))],
        compiler_params=params(),
        cost_estimate=cost(1),
        name="packed",
    )(parts)


def inverted(mine, other, count):
    def kernel(*refs):
        inverse_kernel(1.0 / count, *refs)

    return pl.pallas_call(
        kernel,
        in_specs=[VMEM, VMEM],
        out_specs=VMEM,
        out_shape=shaped((M, M)),
        scratch_shapes=[pltpu.VMEM((M, M), F32)],
        compiler_params=params(),
        cost_estimate=cost(16),
        name="inverted",
    )(mine, other)


def finished(inverse, tiles, z, count):
    own = z.shape[0]
    n = 4
    lines = own // n

    def kernel(*refs):
        finish_kernel(1.0 / count, *refs)

    return pl.pallas_call(
        kernel,
        in_specs=[VMEM, VMEM, HBM],
        out_specs=[VMEM, HBM],
        out_shape=[shaped((M, M)), shaped((own, M))],
        scratch_shapes=[
            pltpu.VMEM((M, M), F32),
            pltpu.VMEM((n, lines, M), BF16),
            pltpu.VMEM((n, lines, M), F32),
            pltpu.SemaphoreType.DMA((2 * n,)),
        ],
        compiler_params=params(),
        cost_estimate=cost(4),
        name="finished",
    )(inverse, tiles, in_hbm(z))


def exchanged(array, axes):
    return lax.all_to_all(array, axes, 0, 0, tiled=True)


def body(samples, freq_table, feature_seeds, phases, treatment_features):
    count = samples.shape[0] * lax.axis_size(ROWS) * lax.axis_size("z")
    turn = lax.axis_size("z")
    rows = lax.axis_size(ROWS)
    x = samples.T
    t = treatment_features.T

    half = turn // 2

    def moved(block, by):
        return lax.ppermute(block, "z", [(k, (k + by) % turn) for k in range(turn)])

    right = {1: moved(x, 1), 2: moved(x, 2)}
    left = {1: moved(x, -1), 2: moved(x, -2)}
    right[3], left[3], right[half] = moved(right[2], 1), moved(left[2], -1), moved(right[2], half - 2)

    freqs, panel, total, z = own_part(freq_table.T, feature_seeds[None, :], phases[None, :], x, t, turn)
    for k in range(1, half):
        total = more_part((-k, k), freqs, panel, total, (right[k], left[k]), t, turn)
    total = more_part((-half,), freqs, panel, total, (right[half],), t, turn, tiled=True)
    parts = exchanged(spread(exchanged(total, ROWS), turn), "z")
    gram, cross = packed(parts, rows)
    mine = exchanged(gram, ROWS[:2])
    inverse = inverted(mine, lax.ppermute(mine, "c", [(0, 1), (1, 0)]), count)
    cross = exchanged(cross, ROWS)
    return finished(inverse, cross, z, count)


def solution(mesh):
    turn = mesh.shape["rhs"]
    torus = Mesh(mesh.devices.reshape(4, 4, 2, turn), ALL)
    placed = (P(ALL, None), P(), P(), P(), P(ROWS, "z"))
    return jax.shard_map(body, mesh=torus, in_specs=placed, out_specs=(P(), P(ALL, None)), check_vma=False)
```

```python
import math

import jax
import jax.numpy as jnp
import numpy as np
from jax import lax
from jax.experimental import pallas as pl
from jax.experimental.pallas import tpu as pltpu
from jax.sharding import Mesh
from jax.sharding import PartitionSpec as P

ROWS = ("y", "x", "c")
ALL = ("y", "x", "c", "z")
RIDGE = 0.05
M = 512
TILE = 128
F32, BF16 = jnp.float32, jnp.bfloat16
MIB = 1 << 20


def sine_coefficients():
    nodes = 0.25 * np.cos(np.pi * (np.arange(400) + 0.5) / 800)
    powers = np.stack([nodes ** (2 * k + 1) for k in range(4)], 1)
    return [float(c) for c in np.linalg.lstsq(powers, np.sqrt(2) * np.sin(2 * np.pi * nodes), rcond=None)[0]]


COEFFS = sine_coefficients()


def split3(a):
    hi = a.astype(BF16)
    rest = a - hi.astype(F32)
    mid = rest.astype(BF16)
    low = (rest - mid.astype(F32)).astype(BF16)
    return hi, mid, low


def split2(a):
    hi = a.astype(BF16)
    return hi, (a - hi.astype(F32)).astype(BF16)


def dot(a, b, ca=1, cb=0):
    return lax.dot_general(a, b, (((ca,), (cb,)), ((), ())), preferred_element_type=F32)


def dot_pieces(a, b, cb=0):
    n = len(a)
    pairs = [(i, j) for i in reversed(range(n)) for j in reversed(range(n - i))]
    return dot(
        jnp.concatenate([a[i] for i, _ in pairs], 1),
        jnp.concatenate([b[j] for _, j in pairs], cb),
        1,
        cb,
    )


def mirrored_product(a, b):
    half = a[0].shape[0] // 2
    upper = dot_pieces([p[:half] for p in a], [p[:, :half] for p in b])
    lower = dot_pieces([p[half:] for p in a], b)
    return jnp.concatenate([jnp.concatenate([upper, lower[:, :half].T], 1), lower], 0)


def select_frequencies(table_ref, seeds_ref, phases_ref):
    seeds = seeds_ref[...]
    near = jnp.bitwise_and(seeds, TILE - 1)
    far = jnp.right_shift(seeds, 7)
    hot = jnp.where(lax.broadcasted_iota(jnp.int32, (TILE, M), 0) == near, 1.0, 0.0).astype(BF16)
    groups = table_ref.shape[1] // TILE
    table = jnp.concatenate([table_ref[:, g * TILE : (g + 1) * TILE] for g in range(groups)], 0)
    pieces = split3(table)
    rows = (dot(pieces[0], hot) + dot(pieces[1], hot)) + dot(pieces[2], hot)
    freqs = jnp.zeros((16, M), F32)
    for g in range(groups):
        freqs = freqs + jnp.where(far == g, rows[g * 16 : (g + 1) * 16], 0.0)
    turns = F32(1 / (2 * math.pi))
    f1, f2, f3 = split3(freqs * turns)
    p1, p2, p3 = (jnp.broadcast_to(p.astype(F32), (16, M)) for p in split3(phases_ref[...] * turns))
    line = lax.broadcasted_iota(jnp.int32, (16, M), 0)
    offset = jnp.where(line == 0, p1, jnp.where(line == 1, p2, jnp.where(line == 2, p3, 0.0))).astype(BF16)
    return jnp.concatenate([f1, f2, f3, f1, f2, f1, offset], 0)


def stacked(x):
    x1, x2, x3 = split3(x)
    return jnp.concatenate([x1, x1, x1, x2, x2, x3, jnp.ones((16, x.shape[1]), BF16)], 0)


def cosines(angle):
    angle = angle - jnp.round(angle)
    q = 0.25 - jnp.abs(angle)
    s = q * q
    p = COEFFS[3] * s + COEFFS[2]
    for c in COEFFS[1::-1]:
        p = p * s + c
    return (p * q).astype(BF16)


CHUNK = 512


def copied(pairs, sems):
    copies = [pltpu.make_async_copy(src, dst, sems.at[k]) for k, (src, dst) in enumerate(pairs)]
    for copy in copies:
        copy.start()
    return copies


def add_block(x, freqs, panel, lhs, z):
    for c in range(0, z.shape[0], CHUNK):
        span = slice(c, c + CHUNK)
        pieces = stacked(x[:, span])
        z[span, :] = cosines(dot(pieces, freqs, 0, 0))
        lhs[lhs.shape[0] - panel.shape[0] :, span] = cosines(dot(panel, pieces))


def block_of(t_hbm, shift, turn, own):
    at = pl.multiple_of(lax.rem(lax.axis_index("z") + shift % turn, turn) * own, own)
    return t_hbm.at[:, pl.ds(at, own)]


def own_kernel(turn, table_hbm, seeds_hbm, phases_hbm, x_hbm, t_hbm, *refs):
    freqs_ref, panel_ref, total_ref, z_hbm, table, seeds, phases, x, z, lhs, sems = refs
    own, cols = z.shape[0], t_hbm.shape[0]
    pairs = [(table_hbm, table), (seeds_hbm, seeds), (phases_hbm, phases), (x_hbm, x)]
    pairs.append((block_of(t_hbm, 0, turn, own), lhs.at[:cols]))
    copies = copied(pairs, sems)
    for copy in copies[:4]:
        copy.wait()
    freqs = select_frequencies(table, seeds, phases)
    freqs_ref[...] = freqs
    wide = panel_ref.shape[0]
    line = lax.broadcasted_iota(jnp.int32, (wide, M), 0) + wide * lax.axis_index("z")
    chosen = jnp.where(line == lax.broadcasted_iota(jnp.int32, (wide, M), 1), 1.0, 0.0).astype(BF16)
    panel = dot(chosen, freqs, 1, 1).astype(BF16)
    panel_ref[...] = panel
    add_block(x, freqs, panel, lhs, z)
    out = pltpu.make_async_copy(z, z_hbm, sems.at[5])
    out.start()
    copies[4].wait()
    total_ref[...] = dot(lhs[...], z[...])
    out.wait()


def more_kernel(shifts, tiled, turn, freqs_ref, panel_ref, before_ref, t_hbm, *refs):
    n = len(shifts)
    xs, (out_ref, lhs, z, sems) = refs[:n], refs[n:]
    own, cols = z.shape[0], t_hbm.shape[0]
    copies = copied([(block_of(t_hbm, s, turn, own), lhs.at[k, :cols]) for k, s in enumerate(shifts)], sems)
    freqs, panel = freqs_ref[...], panel_ref[...]
    total = before_ref[...]
    for k, x_ref in enumerate(xs):
        add_block(x_ref, freqs, panel, lhs.at[k], z)
        copies[k].wait()
        total = total + dot(lhs[k], z[...])
    if tiled:
        across = M // TILE
        for r in range(out_ref.shape[0]):
            i, j = divmod(r, across)
            lanes = slice(TILE * j, TILE * (j + 1))
            out_ref[r, :8] = total[cols + 8 * i : cols + 8 * i + 8, lanes]
            out_ref[r, 8:] = total[8 * i : 8 * i + 8, lanes]
    else:
        out_ref[...] = total


PANELS = 6


def panel_of(block, k):
    return 2 * ((block + k // 2) % (M // TILE)) + k % 2


def pack_kernel(parts_ref, gram_ref, cross_ref):
    column = (2 * lax.axis_index("x") + lax.axis_index("c")) % (M // TILE)
    for k in range(PANELS):
        tile = parts_ref[panel_of(column, k)][:8]
        for r in range(gram_ref.shape[0]):
            gram_ref[r, k] = tile
    for z in range(parts_ref.shape[0]):
        tile = parts_ref[z, 8:]
        for r in range(cross_ref.shape[0]):
            cross_ref[r, z] = tile


def spread_kernel(parts, out_ref):
    total = parts[0]
    for k in range(1, parts.shape[0]):
        total = total + parts[k]
    for k in range(out_ref.shape[0]):
        out_ref[k] = total


def inverse_kernel(scale, mine_ref, other_ref, gram_ref, inverse_ref, error_ref, scale_ref):
    scale_ref[...] = jnp.full(scale_ref.shape, scale, F32)
    across = M // TILE
    core = lax.axis_index("c")
    for r in range(2 * mine_ref.shape[0]):
        i, j = divmod(r, across)
        for k in range(PANELS):
            first = 64 * panel_of(j, k) + 8 * i
            tile = jnp.where(core == r % 2, mine_ref[r // 2, k], other_ref[r // 2, k])
            gram_ref[first : first + 8, TILE * j : TILE * (j + 1)] = tile * scale
    for i in range(across):
        j = (i + 1) % across
        lower = slice(TILE * i, TILE * (i + 1)), slice(TILE * j, TILE * (j + 1))
        gram_ref[lower] = gram_ref[lower[::-1]].T
    eye = identity()
    gram = gram_ref[...] + RIDGE * eye
    gram_ref[...] = gram
    g = split2(gram)
    square = mirrored_product(g, g)

    def bound(matrix):
        return jnp.max(jnp.sum(jnp.abs(matrix), axis=0, keepdims=True), axis=1, keepdims=True)

    top = jnp.minimum(bound(gram), jnp.sqrt(bound(square)) * 1.0001)
    low = jnp.full((1, 1), RIDGE * 0.999, F32)
    m, c = 2.0 / (top - low), (top + low) / (top - low)
    c2, c3, c4 = c * c, c * c * c, c * c * c * c
    last = 16.0 * c4 * c - 20.0 * c3 + 5.0 * c
    p = (
        (80.0 * c4 - 60.0 * c2 + 5.0) * m / last,
        (60.0 * c - 160.0 * c3) * m * m / last,
        (160.0 * c2 - 20.0) * m * m * m / last,
        -80.0 * c * m * m * m * m / last,
        16.0 * m * m * m * m * m / last,
    )
    factor = p[2] * eye + p[3] * gram + p[4] * square
    inverse_ref[...] = p[0] * eye + p[1] * gram + mirrored_product(split2(square), split2(factor))
    error = improved(inverse_ref, g, 1.0 / last, 0.15)
    error_ref[...] = jnp.broadcast_to(error, error_ref.shape)


def identity():
    line = lax.broadcasted_iota(jnp.int32, (M, M), 0)
    lane = lax.broadcasted_iota(jnp.int32, (M, M), 1)
    return jnp.where(line == lane, F32(1), F32(0))


def improved(inverse_ref, g, error, goal):
    twice = 2.0 * identity()

    def more(error):
        return jnp.max(error) > goal

    def step(error):
        gain = 2.0 / (2.0 - error * error)
        pieces = split2(inverse_ref[...])
        rest = twice - dot_pieces(g, pieces)
        inverse_ref[...] = gain * mirrored_product(pieces, split2(rest))
        return error * error * 0.5 * gain

    return lax.while_loop(more, step, error)


def polish_kernel(after_ref, gram_ref, start_ref, error_ref, inverse_ref):
    gram = gram_ref[...]
    inverse_ref[...] = start_ref[...]
    improved(inverse_ref, split2(gram), error_ref[:1, :1], 1e-2)
    x = inverse_ref[...]
    rest = identity() - dot_pieces(split3(gram), split3(x))
    low = rest.astype(BF16)
    rest = rest + dot(low, low)
    inverse_ref[...] = x + dot_pieces(split2(x), split2(rest))


def finish_kernel(inverse_ref, mine_ref, other_ref, z_hbm, coef_ref, fitted_hbm, cross_ref, z, fitted, sems):
    n = z.shape[0]
    lines = z.shape[1]
    spans = [pl.ds(k * lines, lines) for k in range(n)]
    copies = copied([(z_hbm.at[span], z.at[k]) for k, span in enumerate(spans)], sems)
    x = split2(inverse_ref[...])
    across = M // TILE
    core = lax.axis_index("c")
    turn = mine_ref.shape[1]
    for r in range(2 * mine_ref.shape[0]):
        i, j = divmod(r, across)
        for k in range(turn):
            first = k * (M // turn) + 8 * i
            tile = jnp.where(core == r % 2, mine_ref[r // 2, k], other_ref[r // 2, k])
            cross_ref[first : first + 8, TILE * j : TILE * (j + 1)] = tile
    coef = dot_pieces(x, split2(cross_ref[...]), 1)
    coef_ref[...] = coef
    low = coef.astype(BF16)
    outs = []
    for k, span in enumerate(spans):
        copies[k].wait()
        fitted[k] = dot(z[k], low)
        out = pltpu.make_async_copy(fitted.at[k], fitted_hbm.at[span], sems.at[n + k])
        out.start()
        outs.append(out)
    for out in outs:
        out.wait()


def cost(us):
    return pl.CostEstimate(flops=int(us * 1.15e9), transcendentals=0, bytes_accessed=0)


def params(mib=48):
    return pltpu.CompilerParams(vmem_limit_bytes=mib * MIB)


def full(shape):
    return pl.BlockSpec(shape, lambda *_: (0,) * len(shape))


def shaped(shape, dtype=F32):
    return jax.ShapeDtypeStruct(shape, dtype)


HBM = pl.BlockSpec(memory_space=pltpu.HBM)
VMEM = pl.BlockSpec(memory_space=pltpu.VMEM)


def in_hbm(array):
    return pltpu.with_memory_space_constraint(array, pltpu.HBM)


def own_part(table, seeds, phases, x, t, turn):
    own, cols = x.shape[1], t.shape[0]
    wide = M // turn
    ins = (table, seeds, phases, x)

    def kernel(*refs):
        own_kernel(turn, *refs)

    return pl.pallas_call(
        kernel,
        in_specs=[HBM] * 5,
        out_specs=[VMEM, VMEM, VMEM, HBM],
        out_shape=[shaped((112, M), BF16), shaped((wide, 112), BF16), shaped((cols + wide, M)), pltpu.HBM((own, M), BF16)],
        scratch_shapes=[pltpu.VMEM(a.shape, a.dtype) for a in ins]
        + [pltpu.VMEM((own, M), BF16), pltpu.VMEM((cols + wide, own), BF16), pltpu.SemaphoreType.DMA((6,))],
        compiler_params=params(),
        cost_estimate=cost(5),
        name="own_part",
    )(*(in_hbm(a) for a in ins), in_hbm(t))


def more_part(shifts, freqs, panel, before, xs, t, turn, tiled=False):
    own, cols = xs[0].shape[1], t.shape[0]
    n = len(xs)
    lines = before.shape[0]
    out = (cols * M // (8 * TILE), 8 * lines // cols, TILE) if tiled else before.shape

    def kernel(*refs):
        more_kernel(shifts, tiled, turn, *refs)

    return pl.pallas_call(
        kernel,
        in_specs=[VMEM, VMEM, VMEM, HBM] + [VMEM] * n,
        out_specs=VMEM,
        out_shape=shaped(out),
        scratch_shapes=[
            pltpu.VMEM((n, lines, own), BF16),
            pltpu.VMEM((own, M), BF16),
            pltpu.SemaphoreType.DMA((n,)),
        ],
        compiler_params=params(),
        cost_estimate=cost(2.6 * n),
        name="more_part",
    )(freqs, panel, before, in_hbm(t), *xs)


def spread(parts, copies):
    return pl.pallas_call(
        spread_kernel,
        in_specs=[VMEM],
        out_specs=VMEM,
        out_shape=shaped((copies, *parts.shape[1:])),
        compiler_params=params(),
        cost_estimate=cost(1),
        name="spread",
    )(parts)


def packed(parts, rows):
    return pl.pallas_call(
        pack_kernel,
        in_specs=[VMEM],
        out_specs=[VMEM, VMEM],
        out_shape=[shaped((rows // 2, PANELS, 8, TILE)), shaped((rows // 2, parts.shape[0], 8, TILE))],
        compiler_params=params(),
        cost_estimate=cost(1),
        name="packed",
    )(parts)


def inverted(mine, other, count):
    def kernel(*refs):
        inverse_kernel(1.0 / count, *refs)

    return pl.pallas_call(
        kernel,
        in_specs=[VMEM, VMEM],
        out_specs=[VMEM] * 4,
        out_shape=[shaped((M, M)), shaped((M, M)), shaped((8, TILE)), shaped((8, TILE))],
        compiler_params=params(),
        cost_estimate=cost(9),
        name="inverted",
    )(mine, other)


def polished(after, gram, start, error):
    return pl.pallas_call(
        polish_kernel,
        in_specs=[pl.BlockSpec(memory_space=pl.ANY)] + [VMEM] * 3,
        out_specs=VMEM,
        out_shape=shaped((M, M)),
        compiler_params=params(),
        cost_estimate=cost(5),
        name="polished",
    )(after, gram, start, error)


def finished(inverse, mine, other, z):
    own = z.shape[0]
    n = 4
    lines = own // n

    return pl.pallas_call(
        finish_kernel,
        in_specs=[VMEM, VMEM, VMEM, HBM],
        out_specs=[VMEM, HBM],
        out_shape=[shaped((M, M)), shaped((own, M))],
        scratch_shapes=[
            pltpu.VMEM((M, M), F32),
            pltpu.VMEM((n, lines, M), BF16),
            pltpu.VMEM((n, lines, M), F32),
            pltpu.SemaphoreType.DMA((2 * n,)),
        ],
        compiler_params=params(),
        cost_estimate=cost(4),
        name="finished",
    )(inverse, mine, other, in_hbm(z))


def exchanged(array, axes):
    return lax.all_to_all(array, axes, 0, 0, tiled=True)


def body(samples, freq_table, feature_seeds, phases, treatment_features):
    count = samples.shape[0] * lax.axis_size(ROWS) * lax.axis_size("z")
    turn = lax.axis_size("z")
    rows = lax.axis_size(ROWS)
    x = samples.T
    t = treatment_features.T

    half = turn // 2

    def moved(block, by):
        return lax.ppermute(block, "z", [(k, (k + by) % turn) for k in range(turn)])

    right = {1: moved(x, 1), 2: moved(x, 2)}
    left = {1: moved(x, -1), 2: moved(x, -2)}
    right[3], left[3], right[half] = moved(right[2], 1), moved(left[2], -1), moved(right[2], half - 2)

    freqs, panel, total, z = own_part(freq_table.T, feature_seeds[None, :], phases[None, :], x, t, turn)
    near = (right[1], left[1], right[2], left[2])
    total = more_part((-1, 1, -2, 2), freqs, panel, total, near, t, turn)
    far = (right[3], left[3], right[half])
    total = more_part((-3, 3, -half), freqs, panel, total, far, t, turn, tiled=True)
    parts = exchanged(spread(exchanged(total, ROWS), turn), "z")
    gram, cross = packed(parts, rows)
    gram = exchanged(gram, ROWS[:2])
    *start, scale = inverted(gram, swapped(gram), count)
    cross = exchanged(cross, ROWS[:2]) * scale
    inverse = polished(cross, *start)
    return finished(inverse, cross, swapped(cross), z)


def swapped(array):
    return lax.ppermute(array, "c", [(0, 1), (1, 0)])


def solution(mesh):
    turn = mesh.shape["rhs"]
    torus = Mesh(mesh.devices.reshape(4, 4, 2, turn), ALL)
    placed = (P(ALL, None), P(), P(), P(), P(ROWS, "z"))
    return jax.shard_map(body, mesh=torus, in_specs=placed, out_specs=(P(), P(ALL, None)), check_vma=False)
```

```python
import math

import jax
import jax.numpy as jnp
import numpy as np
from jax import lax
from jax.experimental import pallas as pl
from jax.experimental.pallas import tpu as pltpu
from jax.sharding import Mesh
from jax.sharding import PartitionSpec as P

ROWS = ("y", "x", "c")
ALL = ("y", "x", "c", "z")
RIDGE = 0.05
M = 512
TILE = 128
F32, BF16 = jnp.float32, jnp.bfloat16
MIB = 1 << 20


def sine_coefficients():
    nodes = 0.25 * np.cos(np.pi * (np.arange(400) + 0.5) / 800)
    powers = np.stack([nodes ** (2 * k + 1) for k in range(4)], 1)
    return [float(c) for c in np.linalg.lstsq(powers, np.sqrt(2) * np.sin(2 * np.pi * nodes), rcond=None)[0]]


COEFFS = sine_coefficients()


def split3(a):
    hi = a.astype(BF16)
    rest = a - hi.astype(F32)
    mid = rest.astype(BF16)
    low = (rest - mid.astype(F32)).astype(BF16)
    return hi, mid, low


def split2(a):
    hi = a.astype(BF16)
    return hi, (a - hi.astype(F32)).astype(BF16)


def dot(a, b, ca=1, cb=0):
    return lax.dot_general(a, b, (((ca,), (cb,)), ((), ())), preferred_element_type=F32)


def dot_pieces(a, b, cb=0):
    n = len(a)
    pairs = [(i, j) for i in reversed(range(n)) for j in reversed(range(n - i))]
    return dot(
        jnp.concatenate([a[i] for i, _ in pairs], 1),
        jnp.concatenate([b[j] for _, j in pairs], cb),
        1,
        cb,
    )


def mirrored_product(a, b):
    half = a[0].shape[0] // 2
    upper = dot_pieces([p[:half] for p in a], [p[:, :half] for p in b])
    lower = dot_pieces([p[half:] for p in a], b)
    return jnp.concatenate([jnp.concatenate([upper, lower[:, :half].T], 1), lower], 0)


def select_frequencies(table_ref, seeds_ref, phases_ref):
    seeds = seeds_ref[...]
    near = jnp.bitwise_and(seeds, TILE - 1)
    far = jnp.right_shift(seeds, 7)
    hot = jnp.where(lax.broadcasted_iota(jnp.int32, (TILE, M), 0) == near, 1.0, 0.0).astype(BF16)
    groups = table_ref.shape[1] // TILE
    table = jnp.concatenate([table_ref[:, g * TILE : (g + 1) * TILE] for g in range(groups)], 0)
    pieces = split3(table)
    rows = (dot(pieces[0], hot) + dot(pieces[1], hot)) + dot(pieces[2], hot)
    freqs = jnp.zeros((16, M), F32)
    for g in range(groups):
        freqs = freqs + jnp.where(far == g, rows[g * 16 : (g + 1) * 16], 0.0)
    turns = F32(1 / (2 * math.pi))
    f1, f2, f3 = split3(freqs * turns)
    p1, p2, p3 = (jnp.broadcast_to(p.astype(F32), (16, M)) for p in split3(phases_ref[...] * turns))
    line = lax.broadcasted_iota(jnp.int32, (16, M), 0)
    offset = jnp.where(line == 0, p1, jnp.where(line == 1, p2, jnp.where(line == 2, p3, 0.0))).astype(BF16)
    return jnp.concatenate([f1, f2, f3, f1, f2, f1, offset], 0)


def stacked(x):
    x1, x2, x3 = split3(x)
    return jnp.concatenate([x1, x1, x1, x2, x2, x3, jnp.ones((16, x.shape[1]), BF16)], 0)


def cosines(angle):
    angle = angle - jnp.round(angle)
    q = 0.25 - jnp.abs(angle)
    s = q * q
    p = COEFFS[3] * s + COEFFS[2]
    for c in COEFFS[1::-1]:
        p = p * s + c
    return (p * q).astype(BF16)


CHUNK = 512


def copied(pairs, sems):
    copies = [pltpu.make_async_copy(src, dst, sems.at[k]) for k, (src, dst) in enumerate(pairs)]
    for copy in copies:
        copy.start()
    return copies


def add_block(x, freqs, panel, lhs, z):
    for c in range(0, z.shape[0], CHUNK):
        span = slice(c, c + CHUNK)
        pieces = stacked(x[:, span])
        z[span, :] = cosines(dot(pieces, freqs, 0, 0))
        lhs[lhs.shape[0] - panel.shape[0] :, span] = cosines(dot(panel, pieces))


def block_of(t_hbm, shift, turn, own):
    at = pl.multiple_of(lax.rem(lax.axis_index("z") + shift % turn, turn) * own, own)
    return t_hbm.at[:, pl.ds(at, own)]


def own_kernel(turn, table_hbm, seeds_hbm, phases_hbm, x_hbm, t_hbm, *refs):
    freqs_ref, panel_ref, total_ref, z_hbm, table, seeds, phases, x, z, lhs, sems = refs
    own, cols = z.shape[0], t_hbm.shape[0]
    pairs = [(table_hbm, table), (seeds_hbm, seeds), (phases_hbm, phases), (x_hbm, x)]
    pairs.append((block_of(t_hbm, 0, turn, own), lhs.at[:cols]))
    copies = copied(pairs, sems)
    for copy in copies[:4]:
        copy.wait()
    freqs = select_frequencies(table, seeds, phases)
    freqs_ref[...] = freqs
    wide = panel_ref.shape[0]
    line = lax.broadcasted_iota(jnp.int32, (wide, M), 0) + wide * lax.axis_index("z")
    chosen = jnp.where(line == lax.broadcasted_iota(jnp.int32, (wide, M), 1), 1.0, 0.0).astype(BF16)
    panel = dot(chosen, freqs, 1, 1).astype(BF16)
    panel_ref[...] = panel
    add_block(x, freqs, panel, lhs, z)
    out = pltpu.make_async_copy(z, z_hbm, sems.at[5])
    out.start()
    copies[4].wait()
    total_ref[...] = dot(lhs[...], z[...])
    out.wait()


def more_kernel(shifts, tiled, turn, freqs_ref, panel_ref, before_ref, t_hbm, *refs):
    n = len(shifts)
    xs, (out_ref, lhs, z, sems) = refs[:n], refs[n:]
    own, cols = z.shape[0], t_hbm.shape[0]
    copies = copied([(block_of(t_hbm, s, turn, own), lhs.at[k, :cols]) for k, s in enumerate(shifts)], sems)
    freqs, panel = freqs_ref[...], panel_ref[...]
    total = before_ref[...]
    for k, x_ref in enumerate(xs):
        add_block(x_ref, freqs, panel, lhs.at[k], z)
        copies[k].wait()
        total = total + dot(lhs[k], z[...])
    if tiled:
        across = M // TILE
        for r in range(out_ref.shape[0]):
            i, j = divmod(r, across)
            lanes = slice(TILE * j, TILE * (j + 1))
            out_ref[r, :8] = total[cols + 8 * i : cols + 8 * i + 8, lanes]
            out_ref[r, 8:] = total[8 * i : 8 * i + 8, lanes]
    else:
        out_ref[...] = total


PANELS = 6


def panel_of(block, k):
    return 2 * ((block + k // 2) % (M // TILE)) + k % 2


def pack_kernel(parts_ref, gram_ref, cross_ref):
    column = (2 * lax.axis_index("x") + lax.axis_index("c")) % (M // TILE)
    for k in range(PANELS):
        tile = parts_ref[panel_of(column, k)][:8]
        for r in range(gram_ref.shape[0]):
            gram_ref[r, k] = tile
    for z in range(parts_ref.shape[0]):
        tile = parts_ref[z, 8:]
        for r in range(cross_ref.shape[0]):
            cross_ref[r, z] = tile


def spread_kernel(parts, out_ref):
    total = parts[0]
    for k in range(1, parts.shape[0]):
        total = total + parts[k]
    for k in range(out_ref.shape[0]):
        out_ref[k] = total


def inverse_kernel(scale, mine_ref, other_ref, gram_ref, inverse_ref, error_ref, top_ref, scale_ref):
    scale_ref[...] = jnp.full(scale_ref.shape, scale, F32)
    across = M // TILE
    core = lax.axis_index("c")
    for r in range(2 * mine_ref.shape[0]):
        i, j = divmod(r, across)
        for k in range(PANELS):
            first = 64 * panel_of(j, k) + 8 * i
            tile = jnp.where(core == r % 2, mine_ref[r // 2, k], other_ref[r // 2, k])
            gram_ref[first : first + 8, TILE * j : TILE * (j + 1)] = tile * scale
    for i in range(across):
        j = (i + 1) % across
        lower = slice(TILE * i, TILE * (i + 1)), slice(TILE * j, TILE * (j + 1))
        gram_ref[lower] = gram_ref[lower[::-1]].T
    eye = identity()
    gram = gram_ref[...] + RIDGE * eye
    gram_ref[...] = gram
    g = split2(gram)
    square = mirrored_product(g, g)

    def bound(matrix):
        return jnp.max(jnp.sum(jnp.abs(matrix), axis=0, keepdims=True), axis=1, keepdims=True)

    top = jnp.minimum(bound(gram), jnp.sqrt(bound(square)) * 1.0001)
    low = jnp.full((1, 1), RIDGE * 0.999, F32)
    m, c = 2.0 / (top - low), (top + low) / (top - low)
    c2, c3, c4 = c * c, c * c * c, c * c * c * c
    last = 16.0 * c4 * c - 20.0 * c3 + 5.0 * c
    p = (
        (80.0 * c4 - 60.0 * c2 + 5.0) * m / last,
        (60.0 * c - 160.0 * c3) * m * m / last,
        (160.0 * c2 - 20.0) * m * m * m / last,
        -80.0 * c * m * m * m * m / last,
        16.0 * m * m * m * m * m / last,
    )
    factor = p[2] * eye + p[3] * gram + p[4] * square
    inverse_ref[...] = p[0] * eye + p[1] * gram + mirrored_product(split2(square), split2(factor))
    error = improved(inverse_ref, g, 1.0 / last, 0.15, quick=True)
    error_ref[...] = jnp.broadcast_to(error, error_ref.shape)
    top_ref[...] = jnp.broadcast_to(top, top_ref.shape)


def identity():
    line = lax.broadcasted_iota(jnp.int32, (M, M), 0)
    lane = lax.broadcasted_iota(jnp.int32, (M, M), 1)
    return jnp.where(line == lane, F32(1), F32(0))


def improved(inverse_ref, g, error, goal, quick=False):
    twice = 2.0 * identity()

    def more(error):
        return jnp.max(error) > goal

    def step(error):
        gain = 2.0 / (2.0 - error * error)
        if quick:
            x = inverse_ref[...].astype(BF16)
            rest = twice - dot(g[0], x)
            inverse_ref[...] = gain * dot(x, rest.astype(BF16))
        else:
            pieces = split2(inverse_ref[...])
            rest = twice - dot_pieces(g, pieces)
            inverse_ref[...] = gain * mirrored_product(pieces, split2(rest))
        return error * error * 0.5 * gain

    return lax.while_loop(more, step, error)


def polish_kernel(after_ref, gram_ref, start_ref, error_ref, top_ref, inverse_ref, rest_ref):
    inverse_ref[...] = start_ref[...]
    improved(inverse_ref, split2(gram_ref[...]), error_ref[:1, :1], 1e-2)

    def residual():
        rest_ref[...] = identity() - dot_pieces(split3(gram_ref[...]), split3(inverse_ref[...]))

    residual()
    size = jnp.sum(jnp.sum(rest_ref[...] * rest_ref[...], axis=0, keepdims=True), axis=1, keepdims=True)
    small = jnp.max(jnp.where(size < 0.04, 1, 0))

    @pl.when(small == 0)
    def _():
        top, low = top_ref[:1, :1], jnp.full((1, 1), RIDGE * 0.999, F32)
        inverse_ref[...] = (2.0 / (top + low)) * identity()
        improved(inverse_ref, split2(gram_ref[...]), (top - low) / (top + low), 2e-3)
        residual()

    x, rest = inverse_ref[...], rest_ref[...]
    low = rest.astype(BF16)
    rest = rest + dot(low, low)
    inverse_ref[...] = x + dot_pieces(split2(x), split2(rest))


def finish_kernel(inverse_ref, mine_ref, other_ref, z_hbm, coef_hbm, fitted_hbm, cross_ref, coef_ref, z, fitted, sems):
    n = z.shape[0]
    lines = z.shape[1]
    spans = [pl.ds(k * lines, lines) for k in range(n)]
    copies = copied([(z_hbm.at[span], z.at[k]) for k, span in enumerate(spans)], sems)
    x = split2(inverse_ref[...])
    across = M // TILE
    core = lax.axis_index("c")
    turn = mine_ref.shape[1]
    for r in range(2 * mine_ref.shape[0]):
        i, j = divmod(r, across)
        for k in range(turn):
            first = k * (M // turn) + 8 * i
            tile = jnp.where(core == r % 2, mine_ref[r // 2, k], other_ref[r // 2, k])
            cross_ref[first : first + 8, TILE * j : TILE * (j + 1)] = tile
    coef = dot_pieces(x, split2(cross_ref[...]), 1)
    coef_ref[...] = coef
    outs = [pltpu.make_async_copy(coef_ref, coef_hbm, sems.at[2 * n])]
    outs[0].start()
    low = coef.astype(BF16)
    for k, span in enumerate(spans):
        copies[k].wait()
        fitted[k] = dot(z[k], low)
        out = pltpu.make_async_copy(fitted.at[k], fitted_hbm.at[span], sems.at[n + k])
        out.start()
        outs.append(out)
    for out in outs:
        out.wait()


def cost(us):
    return pl.CostEstimate(flops=int(us * 1.15e9), transcendentals=0, bytes_accessed=0)


def params(mib=48):
    return pltpu.CompilerParams(vmem_limit_bytes=mib * MIB)


def full(shape):
    return pl.BlockSpec(shape, lambda *_: (0,) * len(shape))


def shaped(shape, dtype=F32):
    return jax.ShapeDtypeStruct(shape, dtype)


HBM = pl.BlockSpec(memory_space=pltpu.HBM)
VMEM = pl.BlockSpec(memory_space=pltpu.VMEM)


def in_hbm(array):
    return pltpu.with_memory_space_constraint(array, pltpu.HBM)


def own_part(table, seeds, phases, x, t, turn):
    own, cols = x.shape[1], t.shape[0]
    wide = M // turn
    ins = (table, seeds, phases, x)

    def kernel(*refs):
        own_kernel(turn, *refs)

    return pl.pallas_call(
        kernel,
        in_specs=[HBM] * 5,
        out_specs=[VMEM, VMEM, VMEM, HBM],
        out_shape=[shaped((112, M), BF16), shaped((wide, 112), BF16), shaped((cols + wide, M)), pltpu.HBM((own, M), BF16)],
        scratch_shapes=[pltpu.VMEM(a.shape, a.dtype) for a in ins]
        + [pltpu.VMEM((own, M), BF16), pltpu.VMEM((cols + wide, own), BF16), pltpu.SemaphoreType.DMA((6,))],
        compiler_params=params(),
        cost_estimate=cost(5),
        name="own_part",
    )(*(in_hbm(a) for a in ins), in_hbm(t))


def more_part(shifts, freqs, panel, before, xs, t, turn, tiled=False):
    own, cols = xs[0].shape[1], t.shape[0]
    n = len(xs)
    lines = before.shape[0]
    out = (cols * M // (8 * TILE), 8 * lines // cols, TILE) if tiled else before.shape

    def kernel(*refs):
        more_kernel(shifts, tiled, turn, *refs)

    return pl.pallas_call(
        kernel,
        in_specs=[VMEM, VMEM, VMEM, HBM] + [VMEM] * n,
        out_specs=VMEM,
        out_shape=shaped(out),
        scratch_shapes=[
            pltpu.VMEM((n, lines, own), BF16),
            pltpu.VMEM((own, M), BF16),
            pltpu.SemaphoreType.DMA((n,)),
        ],
        compiler_params=params(),
        cost_estimate=cost(2.6 * n),
        name="more_part",
    )(freqs, panel, before, in_hbm(t), *xs)


def spread(parts, copies):
    return pl.pallas_call(
        spread_kernel,
        in_specs=[VMEM],
        out_specs=VMEM,
        out_shape=shaped((copies, *parts.shape[1:])),
        compiler_params=params(),
        cost_estimate=cost(1),
        name="spread",
    )(parts)


def packed(parts, rows):
    return pl.pallas_call(
        pack_kernel,
        in_specs=[VMEM],
        out_specs=[VMEM, VMEM],
        out_shape=[shaped((rows // 2, PANELS, 8, TILE)), shaped((rows // 2, parts.shape[0], 8, TILE))],
        compiler_params=params(),
        cost_estimate=cost(1),
        name="packed",
    )(parts)


def inverted(mine, other, count):
    def kernel(*refs):
        inverse_kernel(1.0 / count, *refs)

    return pl.pallas_call(
        kernel,
        in_specs=[VMEM, VMEM],
        out_specs=[VMEM] * 5,
        out_shape=[shaped((M, M))] * 2 + [shaped((8, TILE))] * 3,
        compiler_params=params(),
        cost_estimate=cost(9),
        name="inverted",
    )(mine, other)


def polished(after, gram, start, error, top):
    return pl.pallas_call(
        polish_kernel,
        in_specs=[pl.BlockSpec(memory_space=pl.ANY)] + [VMEM] * 4,
        out_specs=VMEM,
        out_shape=shaped((M, M)),
        scratch_shapes=[pltpu.VMEM((M, M), F32)],
        compiler_params=params(),
        cost_estimate=cost(5),
        name="polished",
    )(after, gram, start, error, top)


def finished(inverse, mine, other, z):
    own = z.shape[0]
    n = 4
    lines = own // n

    return pl.pallas_call(
        finish_kernel,
        in_specs=[VMEM, VMEM, VMEM, HBM],
        out_specs=[HBM, HBM],
        out_shape=[shaped((M, M)), shaped((own, M))],
        scratch_shapes=[
            pltpu.VMEM((M, M), F32),
            pltpu.VMEM((M, M), F32),
            pltpu.VMEM((n, lines, M), BF16),
            pltpu.VMEM((n, lines, M), F32),
            pltpu.SemaphoreType.DMA((2 * n + 1,)),
        ],
        compiler_params=params(),
        cost_estimate=cost(4),
        name="finished",
    )(inverse, mine, other, in_hbm(z))


def exchanged(array, axes):
    return lax.all_to_all(array, axes, 0, 0, tiled=True)


def body(samples, freq_table, feature_seeds, phases, treatment_features):
    count = samples.shape[0] * lax.axis_size(ROWS) * lax.axis_size("z")
    turn = lax.axis_size("z")
    rows = lax.axis_size(ROWS)
    x = samples.T
    t = treatment_features.T

    half = turn // 2

    def moved(block, by):
        return lax.ppermute(block, "z", [(k, (k + by) % turn) for k in range(turn)])

    right = {1: moved(x, 1), 2: moved(x, 2)}
    left = {1: moved(x, -1), 2: moved(x, -2)}
    right[3], left[3], right[half] = moved(right[2], 1), moved(left[2], -1), moved(right[2], half - 2)

    freqs, panel, total, z = own_part(freq_table.T, feature_seeds[None, :], phases[None, :], x, t, turn)
    near = (right[1], left[1], right[2], left[2])
    total = more_part((-1, 1, -2, 2), freqs, panel, total, near, t, turn)
    far = (right[3], left[3], right[half])
    total = more_part((-3, 3, -half), freqs, panel, total, far, t, turn, tiled=True)
    parts = exchanged(spread(exchanged(total, ROWS), turn), "z")
    gram, cross = packed(parts, rows)
    gram = exchanged(gram, ROWS[:2])
    *start, scale = inverted(gram, swapped(gram), count)
    cross = exchanged(cross, ROWS[:2]) * scale
    inverse = polished(cross, *start)
    return finished(inverse, cross, swapped(cross), z)


def swapped(array):
    return lax.ppermute(array, "c", [(0, 1), (1, 0)])


def solution(mesh):
    turn = mesh.shape["rhs"]
    torus = Mesh(mesh.devices.reshape(4, 4, 2, turn), ALL)
    placed = (P(ALL, None), P(), P(), P(), P(ROWS, "z"))
    return jax.shard_map(body, mesh=torus, in_specs=placed, out_specs=(P(), P(ALL, None)), check_vma=False)
```

```python
import math

import jax
import jax.numpy as jnp
import numpy as np
from jax import lax
from jax.experimental import pallas as pl
from jax.experimental.pallas import tpu as pltpu
from jax.sharding import Mesh
from jax.sharding import PartitionSpec as P

ROWS = ("y", "x", "c")
ALL = ("y", "x", "c", "z")
RIDGE = 0.05
M = 512
TILE = 128
F32, BF16 = jnp.float32, jnp.bfloat16
MIB = 1 << 20


def sine_coefficients():
    nodes = 0.25 * np.cos(np.pi * (np.arange(400) + 0.5) / 800)
    powers = np.stack([nodes ** (2 * k + 1) for k in range(4)], 1)
    return [float(c) for c in np.linalg.lstsq(powers, np.sqrt(2) * np.sin(2 * np.pi * nodes), rcond=None)[0]]


COEFFS = sine_coefficients()


def split3(a):
    hi = a.astype(BF16)
    rest = a - hi.astype(F32)
    mid = rest.astype(BF16)
    low = (rest - mid.astype(F32)).astype(BF16)
    return hi, mid, low


def split2(a):
    hi = a.astype(BF16)
    return hi, (a - hi.astype(F32)).astype(BF16)


def dot(a, b, ca=1, cb=0):
    return lax.dot_general(a, b, (((ca,), (cb,)), ((), ())), preferred_element_type=F32)


def dot_pieces(a, b, cb=0):
    n = len(a)
    pairs = [(i, j) for i in reversed(range(n)) for j in reversed(range(n - i))]
    return dot(
        jnp.concatenate([a[i] for i, _ in pairs], 1),
        jnp.concatenate([b[j] for _, j in pairs], cb),
        1,
        cb,
    )


def mirrored_product(a, b):
    half = a[0].shape[0] // 2
    upper = dot_pieces([p[:half] for p in a], [p[:, :half] for p in b])
    lower = dot_pieces([p[half:] for p in a], b)
    return jnp.concatenate([jnp.concatenate([upper, lower[:, :half].T], 1), lower], 0)


def select_frequencies(table_ref, seeds_ref, phases_ref):
    seeds = seeds_ref[...]
    near = jnp.bitwise_and(seeds, TILE - 1)
    far = jnp.right_shift(seeds, 7)
    hot = jnp.where(lax.broadcasted_iota(jnp.int32, (TILE, M), 0) == near, 1.0, 0.0).astype(BF16)
    groups = table_ref.shape[1] // TILE
    table = jnp.concatenate([table_ref[:, g * TILE : (g + 1) * TILE] for g in range(groups)], 0)
    pieces = split3(table)
    rows = (dot(pieces[0], hot) + dot(pieces[1], hot)) + dot(pieces[2], hot)
    freqs = jnp.zeros((16, M), F32)
    for g in range(groups):
        freqs = freqs + jnp.where(far == g, rows[g * 16 : (g + 1) * 16], 0.0)
    turns = F32(1 / (2 * math.pi))
    f1, f2, f3 = split3(freqs * turns)
    p1, p2, p3 = (jnp.broadcast_to(p.astype(F32), (16, M)) for p in split3(phases_ref[...] * turns))
    line = lax.broadcasted_iota(jnp.int32, (16, M), 0)
    offset = jnp.where(line == 0, p1, jnp.where(line == 1, p2, jnp.where(line == 2, p3, 0.0))).astype(BF16)
    return jnp.concatenate([f1, f2, f3, f1, f2, f1, offset], 0)


def stacked(x):
    x1, x2, x3 = split3(x)
    return jnp.concatenate([x1, x1, x1, x2, x2, x3, jnp.ones((16, x.shape[1]), BF16)], 0)


def cosines(angle):
    angle = angle - jnp.round(angle)
    q = 0.25 - jnp.abs(angle)
    s = q * q
    p = COEFFS[3] * s + COEFFS[2]
    for c in COEFFS[1::-1]:
        p = p * s + c
    return (p * q).astype(BF16)


CHUNK = 512


def copied(pairs, sems):
    copies = [pltpu.make_async_copy(src, dst, sems.at[k]) for k, (src, dst) in enumerate(pairs)]
    for copy in copies:
        copy.start()
    return copies


def add_block(x, freqs, panel, lhs, z):
    for c in range(0, z.shape[0], CHUNK):
        span = slice(c, c + CHUNK)
        pieces = stacked(x[:, span])
        z[span, :] = cosines(dot(pieces, freqs, 0, 0))
        lhs[lhs.shape[0] - panel.shape[0] :, span] = cosines(dot(panel, pieces))


def block_of(t_hbm, shift, turn, own):
    at = pl.multiple_of(lax.rem(lax.axis_index("z") + shift % turn, turn) * own, own)
    return t_hbm.at[:, pl.ds(at, own)]


def own_kernel(turn, table_hbm, seeds_hbm, phases_hbm, x_hbm, t_hbm, *refs):
    freqs_ref, panel_ref, total_ref, z_hbm, table, seeds, phases, x, z, lhs, sems = refs
    own, cols = z.shape[0], t_hbm.shape[0]
    pairs = [(table_hbm, table), (seeds_hbm, seeds), (phases_hbm, phases), (x_hbm, x)]
    pairs.append((block_of(t_hbm, 0, turn, own), lhs.at[:cols]))
    copies = copied(pairs, sems)
    for copy in copies[:4]:
        copy.wait()
    freqs = select_frequencies(table, seeds, phases)
    freqs_ref[...] = freqs
    wide = panel_ref.shape[0]
    line = lax.broadcasted_iota(jnp.int32, (wide, M), 0) + wide * lax.axis_index("z")
    chosen = jnp.where(line == lax.broadcasted_iota(jnp.int32, (wide, M), 1), 1.0, 0.0).astype(BF16)
    panel = dot(chosen, freqs, 1, 1).astype(BF16)
    panel_ref[...] = panel
    add_block(x, freqs, panel, lhs, z)
    out = pltpu.make_async_copy(z, z_hbm, sems.at[5])
    out.start()
    copies[4].wait()
    total_ref[...] = dot(lhs[...], z[...])
    out.wait()


def more_kernel(shifts, tiled, turn, freqs_ref, panel_ref, before_ref, t_hbm, *refs):
    n = len(shifts)
    xs, (out_ref, lhs, z, sems) = refs[:n], refs[n:]
    own, cols = z.shape[0], t_hbm.shape[0]
    copies = copied([(block_of(t_hbm, s, turn, own), lhs.at[k, :cols]) for k, s in enumerate(shifts)], sems)
    freqs, panel = freqs_ref[...], panel_ref[...]
    total = before_ref[...]
    for k, x_ref in enumerate(xs):
        add_block(x_ref, freqs, panel, lhs.at[k], z)
        copies[k].wait()
        total = total + dot(lhs[k], z[...])
    if tiled:
        across = M // TILE
        for r in range(out_ref.shape[0]):
            i, j = divmod(r, across)
            lanes = slice(TILE * j, TILE * (j + 1))
            out_ref[r, :8] = total[cols + 8 * i : cols + 8 * i + 8, lanes]
            out_ref[r, 8:] = total[8 * i : 8 * i + 8, lanes]
    else:
        out_ref[...] = total


PANELS = 6


def panel_of(block, k):
    return 2 * ((block + k // 2) % (M // TILE)) + k % 2


def pack_kernel(parts_ref, gram_ref, cross_ref):
    column = (2 * lax.axis_index("x") + lax.axis_index("c")) % (M // TILE)
    for k in range(PANELS):
        tile = parts_ref[panel_of(column, k)][:8]
        for r in range(gram_ref.shape[0]):
            gram_ref[r, k] = tile
    for z in range(parts_ref.shape[0]):
        tile = parts_ref[z, 8:]
        for r in range(cross_ref.shape[0]):
            cross_ref[r, z] = tile


def spread_kernel(parts, out_ref):
    total = parts[0]
    for k in range(1, parts.shape[0]):
        total = total + parts[k]
    for k in range(out_ref.shape[0]):
        out_ref[k] = total


def inverse_kernel(scale, mine_ref, other_ref, gram_ref, inverse_ref, top_ref, scale_ref):
    scale_ref[...] = jnp.full(scale_ref.shape, scale, F32)
    across = M // TILE
    core = lax.axis_index("c")
    for r in range(2 * mine_ref.shape[0]):
        i, j = divmod(r, across)
        for k in range(PANELS):
            first = 64 * panel_of(j, k) + 8 * i
            tile = jnp.where(core == r % 2, mine_ref[r // 2, k], other_ref[r // 2, k])
            gram_ref[first : first + 8, TILE * j : TILE * (j + 1)] = tile * scale
    for i in range(across):
        j = (i + 1) % across
        lower = slice(TILE * i, TILE * (i + 1)), slice(TILE * j, TILE * (j + 1))
        gram_ref[lower] = gram_ref[lower[::-1]].T
    eye = identity()
    gram = gram_ref[...] + RIDGE * eye
    gram_ref[...] = gram
    g = split2(gram)
    square = mirrored_product(g, g)

    def bound(matrix):
        return jnp.max(jnp.sum(jnp.abs(matrix), axis=0, keepdims=True), axis=1, keepdims=True)

    top = jnp.minimum(bound(gram), jnp.sqrt(bound(square)) * 1.0001)
    low = jnp.full((1, 1), RIDGE * 0.999, F32)
    m, c = 2.0 / (top - low), (top + low) / (top - low)
    c2, c3, c4 = c * c, c * c * c, c * c * c * c
    last = 16.0 * c4 * c - 20.0 * c3 + 5.0 * c
    p = (
        (80.0 * c4 - 60.0 * c2 + 5.0) * m / last,
        (60.0 * c - 160.0 * c3) * m * m / last,
        (160.0 * c2 - 20.0) * m * m * m / last,
        -80.0 * c * m * m * m * m / last,
        16.0 * m * m * m * m * m / last,
    )
    factor = p[2] * eye + p[3] * gram + p[4] * square
    inverse_ref[...] = p[0] * eye + p[1] * gram + mirrored_product(split2(square), split2(factor))
    error = improved(inverse_ref, g, 1.0 / last, 0.15, quick=True)
    improved(inverse_ref, g, error, 1e-2)
    top_ref[...] = jnp.broadcast_to(top, top_ref.shape)


def identity():
    line = lax.broadcasted_iota(jnp.int32, (M, M), 0)
    lane = lax.broadcasted_iota(jnp.int32, (M, M), 1)
    return jnp.where(line == lane, F32(1), F32(0))


def improved(inverse_ref, g, error, goal, quick=False):
    twice = 2.0 * identity()

    def more(error):
        return jnp.max(error) > goal

    def step(error):
        gain = 2.0 / (2.0 - error * error)
        if quick:
            x = inverse_ref[...].astype(BF16)
            rest = twice - dot(g[0], x)
            inverse_ref[...] = gain * dot(x, rest.astype(BF16))
        else:
            pieces = split2(inverse_ref[...])
            rest = twice - dot_pieces(g, pieces)
            inverse_ref[...] = gain * mirrored_product(pieces, split2(rest))
        return error * error * 0.5 * gain

    return lax.while_loop(more, step, error)


def polish_kernel(after_ref, gram_ref, start_ref, top_ref, inverse_ref, rest_ref):
    inverse_ref[...] = start_ref[...]

    def residual():
        rest_ref[...] = identity() - dot_pieces(split3(gram_ref[...]), split3(inverse_ref[...]))

    residual()
    size = jnp.sum(jnp.sum(rest_ref[...] * rest_ref[...], axis=0, keepdims=True), axis=1, keepdims=True)
    small = jnp.max(jnp.where(size < 0.04, 1, 0))

    @pl.when(small == 0)
    def _():
        top, low = top_ref[:1, :1], jnp.full((1, 1), RIDGE * 0.999, F32)
        inverse_ref[...] = (2.0 / (top + low)) * identity()
        improved(inverse_ref, split2(gram_ref[...]), (top - low) / (top + low), 2e-3)
        residual()

    x, rest = inverse_ref[...], rest_ref[...]
    low = rest.astype(BF16)
    rest = rest + dot(low, low)
    inverse_ref[...] = x + dot_pieces(split2(x), split2(rest))


def finish_kernel(inverse_ref, mine_ref, other_ref, z_hbm, coef_hbm, fitted_hbm, cross_ref, coef_ref, z, fitted, sems):
    n = z.shape[0]
    lines = z.shape[1]
    spans = [pl.ds(k * lines, lines) for k in range(n)]
    copies = copied([(z_hbm.at[span], z.at[k]) for k, span in enumerate(spans)], sems)
    x = split2(inverse_ref[...])
    across = M // TILE
    core = lax.axis_index("c")
    turn = mine_ref.shape[1]
    for r in range(2 * mine_ref.shape[0]):
        i, j = divmod(r, across)
        for k in range(turn):
            first = k * (M // turn) + 8 * i
            tile = jnp.where(core == r % 2, mine_ref[r // 2, k], other_ref[r // 2, k])
            cross_ref[first : first + 8, TILE * j : TILE * (j + 1)] = tile
    coef = dot_pieces(x, split2(cross_ref[...]), 1)
    coef_ref[...] = coef
    outs = [pltpu.make_async_copy(coef_ref, coef_hbm, sems.at[2 * n])]
    outs[0].start()
    low = coef.astype(BF16)
    for k, span in enumerate(spans):
        copies[k].wait()
        fitted[k] = dot(z[k], low)
        out = pltpu.make_async_copy(fitted.at[k], fitted_hbm.at[span], sems.at[n + k])
        out.start()
        outs.append(out)
    for out in outs:
        out.wait()


def cost(us):
    return pl.CostEstimate(flops=int(us * 1.15e9), transcendentals=0, bytes_accessed=0)


def params(mib=48):
    return pltpu.CompilerParams(vmem_limit_bytes=mib * MIB)


def full(shape):
    return pl.BlockSpec(shape, lambda *_: (0,) * len(shape))


def shaped(shape, dtype=F32):
    return jax.ShapeDtypeStruct(shape, dtype)


HBM = pl.BlockSpec(memory_space=pltpu.HBM)
VMEM = pl.BlockSpec(memory_space=pltpu.VMEM)


def in_hbm(array):
    return pltpu.with_memory_space_constraint(array, pltpu.HBM)


def own_part(table, seeds, phases, x, t, turn):
    own, cols = x.shape[1], t.shape[0]
    wide = M // turn
    ins = (table, seeds, phases, x)

    def kernel(*refs):
        own_kernel(turn, *refs)

    return pl.pallas_call(
        kernel,
        in_specs=[HBM] * 5,
        out_specs=[VMEM, VMEM, VMEM, HBM],
        out_shape=[shaped((112, M), BF16), shaped((wide, 112), BF16), shaped((cols + wide, M)), pltpu.HBM((own, M), BF16)],
        scratch_shapes=[pltpu.VMEM(a.shape, a.dtype) for a in ins]
        + [pltpu.VMEM((own, M), BF16), pltpu.VMEM((cols + wide, own), BF16), pltpu.SemaphoreType.DMA((6,))],
        compiler_params=params(),
        cost_estimate=cost(5),
        name="own_part",
    )(*(in_hbm(a) for a in ins), in_hbm(t))


def more_part(shifts, freqs, panel, before, xs, t, turn, tiled=False):
    own, cols = xs[0].shape[1], t.shape[0]
    n = len(xs)
    lines = before.shape[0]
    out = (cols * M // (8 * TILE), 8 * lines // cols, TILE) if tiled else before.shape

    def kernel(*refs):
        more_kernel(shifts, tiled, turn, *refs)

    return pl.pallas_call(
        kernel,
        in_specs=[VMEM, VMEM, VMEM, HBM] + [VMEM] * n,
        out_specs=VMEM,
        out_shape=shaped(out),
        scratch_shapes=[
            pltpu.VMEM((n, lines, own), BF16),
            pltpu.VMEM((own, M), BF16),
            pltpu.SemaphoreType.DMA((n,)),
        ],
        compiler_params=params(),
        cost_estimate=cost(2.6 * n),
        name="more_part",
    )(freqs, panel, before, in_hbm(t), *xs)


def spread(parts, copies):
    return pl.pallas_call(
        spread_kernel,
        in_specs=[VMEM],
        out_specs=VMEM,
        out_shape=shaped((copies, *parts.shape[1:])),
        compiler_params=params(),
        cost_estimate=cost(1),
        name="spread",
    )(parts)


def packed(parts, rows):
    return pl.pallas_call(
        pack_kernel,
        in_specs=[VMEM],
        out_specs=[VMEM, VMEM],
        out_shape=[shaped((rows // 2, PANELS, 8, TILE)), shaped((rows // 2, parts.shape[0], 8, TILE))],
        compiler_params=params(),
        cost_estimate=cost(1),
        name="packed",
    )(parts)


def inverted(mine, other, count):
    def kernel(*refs):
        inverse_kernel(1.0 / count, *refs)

    return pl.pallas_call(
        kernel,
        in_specs=[VMEM, VMEM],
        out_specs=[VMEM] * 4,
        out_shape=[shaped((M, M))] * 2 + [shaped((8, TILE))] * 2,
        compiler_params=params(),
        cost_estimate=cost(9),
        name="inverted",
    )(mine, other)


def polished(after, gram, start, top):
    return pl.pallas_call(
        polish_kernel,
        in_specs=[pl.BlockSpec(memory_space=pl.ANY)] + [VMEM] * 3,
        out_specs=VMEM,
        out_shape=shaped((M, M)),
        scratch_shapes=[pltpu.VMEM((M, M), F32)],
        compiler_params=params(),
        cost_estimate=cost(5),
        name="polished",
    )(after, gram, start, top)


def finished(inverse, mine, other, z):
    own = z.shape[0]
    n = 4
    lines = own // n

    return pl.pallas_call(
        finish_kernel,
        in_specs=[VMEM, VMEM, VMEM, HBM],
        out_specs=[HBM, HBM],
        out_shape=[shaped((M, M)), shaped((own, M))],
        scratch_shapes=[
            pltpu.VMEM((M, M), F32),
            pltpu.VMEM((M, M), F32),
            pltpu.VMEM((n, lines, M), BF16),
            pltpu.VMEM((n, lines, M), F32),
            pltpu.SemaphoreType.DMA((2 * n + 1,)),
        ],
        compiler_params=params(),
        cost_estimate=cost(4),
        name="finished",
    )(inverse, mine, other, in_hbm(z))


def exchanged(array, axes):
    return lax.all_to_all(array, axes, 0, 0, tiled=True)


def body(samples, freq_table, feature_seeds, phases, treatment_features):
    count = samples.shape[0] * lax.axis_size(ROWS) * lax.axis_size("z")
    turn = lax.axis_size("z")
    rows = lax.axis_size(ROWS)
    x = samples.T
    t = treatment_features.T

    half = turn // 2

    def moved(block, by):
        return lax.ppermute(block, "z", [(k, (k + by) % turn) for k in range(turn)])

    right = {1: moved(x, 1), 2: moved(x, 2)}
    left = {1: moved(x, -1), 2: moved(x, -2)}
    right[3], left[3], right[half] = moved(right[2], 1), moved(left[2], -1), moved(right[2], half - 2)

    freqs, panel, total, z = own_part(freq_table.T, feature_seeds[None, :], phases[None, :], x, t, turn)
    near = (right[1], left[1], right[2], left[2])
    total = more_part((-1, 1, -2, 2), freqs, panel, total, near, t, turn)
    far = (right[3], left[3], right[half])
    total = more_part((-3, 3, -half), freqs, panel, total, far, t, turn, tiled=True)
    parts = exchanged(spread(exchanged(total, ROWS), turn), "z")
    gram, cross = packed(parts, rows)
    gram = exchanged(gram, ROWS[:2])
    *start, scale = inverted(gram, swapped(gram), count)
    cross = exchanged(cross, ROWS[:2]) * scale
    inverse = polished(cross, *start)
    return finished(inverse, cross, swapped(cross), z)


def swapped(array):
    return lax.ppermute(array, "c", [(0, 1), (1, 0)])


def solution(mesh):
    turn = mesh.shape["rhs"]
    torus = Mesh(mesh.devices.reshape(4, 4, 2, turn), ALL)
    placed = (P(ALL, None), P(), P(), P(), P(ROWS, "z"))
    return jax.shard_map(body, mesh=torus, in_specs=placed, out_specs=(P(), P(ALL, None)), check_vma=False)
```

```python
import math

import jax
import jax.numpy as jnp
import numpy as np
from jax import lax
from jax.experimental import pallas as pl
from jax.experimental.pallas import tpu as pltpu
from jax.sharding import Mesh
from jax.sharding import PartitionSpec as P

ROWS = ("y", "x", "c")
ALL = ("y", "x", "c", "z")
RIDGE = 0.05
M = 512
TILE = 128
F32, BF16 = jnp.float32, jnp.bfloat16
MIB = 1 << 20


def sine_coefficients():
    nodes = 0.25 * np.cos(np.pi * (np.arange(400) + 0.5) / 800)
    powers = np.stack([nodes ** (2 * k + 1) for k in range(4)], 1)
    return [float(c) for c in np.linalg.lstsq(powers, np.sqrt(2) * np.sin(2 * np.pi * nodes), rcond=None)[0]]


COEFFS = sine_coefficients()


def split3(a):
    hi = a.astype(BF16)
    rest = a - hi.astype(F32)
    mid = rest.astype(BF16)
    low = (rest - mid.astype(F32)).astype(BF16)
    return hi, mid, low


def split2(a):
    hi = a.astype(BF16)
    return hi, (a - hi.astype(F32)).astype(BF16)


def dot(a, b, ca=1, cb=0):
    return lax.dot_general(a, b, (((ca,), (cb,)), ((), ())), preferred_element_type=F32)


def dot_pieces(a, b, cb=0):
    n = len(a)
    pairs = [(i, j) for i in reversed(range(n)) for j in reversed(range(n - i))]
    return dot(
        jnp.concatenate([a[i] for i, _ in pairs], 1),
        jnp.concatenate([b[j] for _, j in pairs], cb),
        1,
        cb,
    )


def mirrored_product(a, b):
    half = a[0].shape[0] // 2
    upper = dot_pieces([p[:half] for p in a], [p[:, :half] for p in b])
    lower = dot_pieces([p[half:] for p in a], b)
    return jnp.concatenate([jnp.concatenate([upper, lower[:, :half].T], 1), lower], 0)


def select_frequencies(table_ref, seeds_ref, phases_ref):
    seeds = seeds_ref[...]
    near = jnp.bitwise_and(seeds, TILE - 1)
    far = jnp.right_shift(seeds, 7)
    hot = jnp.where(lax.broadcasted_iota(jnp.int32, (TILE, M), 0) == near, 1.0, 0.0).astype(BF16)
    groups = table_ref.shape[1] // TILE
    table = jnp.concatenate([table_ref[:, g * TILE : (g + 1) * TILE] for g in range(groups)], 0)
    pieces = split3(table)
    rows = (dot(pieces[0], hot) + dot(pieces[1], hot)) + dot(pieces[2], hot)
    freqs = jnp.zeros((16, M), F32)
    for g in range(groups):
        freqs = freqs + jnp.where(far == g, rows[g * 16 : (g + 1) * 16], 0.0)
    turns = F32(1 / (2 * math.pi))
    f1, f2, f3 = split3(freqs * turns)
    p1, p2, p3 = (jnp.broadcast_to(p.astype(F32), (16, M)) for p in split3(phases_ref[...] * turns))
    line = lax.broadcasted_iota(jnp.int32, (16, M), 0)
    offset = jnp.where(line == 0, p1, jnp.where(line == 1, p2, jnp.where(line == 2, p3, 0.0))).astype(BF16)
    return jnp.concatenate([f1, f2, f3, f1, f2, f1, offset], 0)


def stacked(x):
    x1, x2, x3 = split3(x)
    return jnp.concatenate([x1, x1, x1, x2, x2, x3, jnp.ones((16, x.shape[1]), BF16)], 0)


def cosines(angle):
    angle = angle - jnp.round(angle)
    q = 0.25 - jnp.abs(angle)
    s = q * q
    p = COEFFS[3] * s + COEFFS[2]
    for c in COEFFS[1::-1]:
        p = p * s + c
    return (p * q).astype(BF16)


CHUNK = 512


def copied(pairs, sems):
    copies = [pltpu.make_async_copy(src, dst, sems.at[k]) for k, (src, dst) in enumerate(pairs)]
    for copy in copies:
        copy.start()
    return copies


def add_block(x, freqs, panel, lhs, z):
    for c in range(0, z.shape[0], CHUNK):
        span = slice(c, c + CHUNK)
        pieces = stacked(x[:, span])
        z[span, :] = cosines(dot(pieces, freqs, 0, 0))
        lhs[lhs.shape[0] - panel.shape[0] :, span] = cosines(dot(panel, pieces))


def block_of(t_hbm, shift, turn, own):
    at = pl.multiple_of(lax.rem(lax.axis_index("z") + shift % turn, turn) * own, own)
    return t_hbm.at[:, pl.ds(at, own)]


def own_kernel(turn, table_hbm, seeds_hbm, phases_hbm, x_hbm, t_hbm, *refs):
    freqs_ref, panel_ref, total_ref, z_hbm, table, seeds, phases, x, z, lhs, sems = refs
    own, cols = z.shape[0], t_hbm.shape[0]
    pairs = [(table_hbm, table), (seeds_hbm, seeds), (phases_hbm, phases), (x_hbm, x)]
    pairs.append((block_of(t_hbm, 0, turn, own), lhs.at[:cols]))
    copies = copied(pairs, sems)
    for copy in copies[:4]:
        copy.wait()
    freqs = select_frequencies(table, seeds, phases)
    freqs_ref[...] = freqs
    wide = panel_ref.shape[0]
    line = lax.broadcasted_iota(jnp.int32, (wide, M), 0) + wide * lax.axis_index("z")
    chosen = jnp.where(line == lax.broadcasted_iota(jnp.int32, (wide, M), 1), 1.0, 0.0).astype(BF16)
    panel = dot(chosen, freqs, 1, 1).astype(BF16)
    panel_ref[...] = panel
    add_block(x, freqs, panel, lhs, z)
    out = pltpu.make_async_copy(z, z_hbm, sems.at[5])
    out.start()
    copies[4].wait()
    total_ref[...] = dot(lhs[...], z[...])
    out.wait()


def more_kernel(shifts, tiled, turn, freqs_ref, panel_ref, before_ref, t_hbm, *refs):
    n = len(shifts)
    xs, (out_ref, lhs, z, sems) = refs[:n], refs[n:]
    own, cols = z.shape[0], t_hbm.shape[0]
    copies = copied([(block_of(t_hbm, s, turn, own), lhs.at[k, :cols]) for k, s in enumerate(shifts)], sems)
    freqs, panel = freqs_ref[...], panel_ref[...]
    total = before_ref[...]
    for k, x_ref in enumerate(xs):
        add_block(x_ref, freqs, panel, lhs.at[k], z)
        copies[k].wait()
        total = total + dot(lhs[k], z[...])
    if tiled:
        across = M // TILE
        for r in range(out_ref.shape[0]):
            i, j = divmod(r, across)
            lanes = slice(TILE * j, TILE * (j + 1))
            out_ref[r, :8] = total[cols + 8 * i : cols + 8 * i + 8, lanes]
            out_ref[r, 8:] = total[8 * i : 8 * i + 8, lanes]
    else:
        out_ref[...] = total


PANELS = 6


def panel_of(block, k):
    return 2 * ((block + k // 2) % (M // TILE)) + k % 2


def pack_kernel(parts_ref, gram_ref, cross_ref):
    column = (2 * lax.axis_index("x") + lax.axis_index("c")) % (M // TILE)
    for k in range(PANELS):
        tile = parts_ref[panel_of(column, k)][:8]
        for r in range(gram_ref.shape[0]):
            gram_ref[r, k] = tile
    for z in range(parts_ref.shape[0]):
        tile = parts_ref[z, 8:]
        for r in range(cross_ref.shape[0]):
            cross_ref[r, z] = tile


def spread_kernel(parts, out_ref):
    total = parts[0]
    for k in range(1, parts.shape[0]):
        total = total + parts[k]
    for k in range(out_ref.shape[0]):
        out_ref[k] = total


def inverse_kernel(scale, mine_ref, other_ref, gram_ref, inverse_ref, scale_ref):
    scale_ref[...] = jnp.full(scale_ref.shape, scale, F32)
    across = M // TILE
    core = lax.axis_index("c")
    for r in range(2 * mine_ref.shape[0]):
        i, j = divmod(r, across)
        for k in range(PANELS):
            first = 64 * panel_of(j, k) + 8 * i
            tile = jnp.where(core == r % 2, mine_ref[r // 2, k], other_ref[r // 2, k])
            gram_ref[first : first + 8, TILE * j : TILE * (j + 1)] = tile * scale
    for i in range(across):
        j = (i + 1) % across
        lower = slice(TILE * i, TILE * (i + 1)), slice(TILE * j, TILE * (j + 1))
        gram_ref[lower] = gram_ref[lower[::-1]].T
    eye = identity()
    gram = gram_ref[...] + RIDGE * eye
    gram_ref[...] = gram
    g = split2(gram)
    square = mirrored_product(g, g)

    def bound(matrix):
        return jnp.max(jnp.sum(jnp.abs(matrix), axis=0, keepdims=True), axis=1, keepdims=True)

    top = jnp.minimum(bound(gram), jnp.sqrt(bound(square)) * 1.0001)
    low = jnp.full((1, 1), RIDGE * 0.999, F32)
    m, c = 2.0 / (top - low), (top + low) / (top - low)
    c2, c3, c4 = c * c, c * c * c, c * c * c * c
    last = 16.0 * c4 * c - 20.0 * c3 + 5.0 * c
    p = (
        (80.0 * c4 - 60.0 * c2 + 5.0) * m / last,
        (60.0 * c - 160.0 * c3) * m * m / last,
        (160.0 * c2 - 20.0) * m * m * m / last,
        -80.0 * c * m * m * m * m / last,
        16.0 * m * m * m * m * m / last,
    )
    factor = p[2] * eye + p[3] * gram + p[4] * square
    inverse_ref[...] = p[0] * eye + p[1] * gram + mirrored_product(split2(square), split2(factor))
    improved(inverse_ref, g, 1.0 / last, 1e-2)


def identity():
    line = lax.broadcasted_iota(jnp.int32, (M, M), 0)
    lane = lax.broadcasted_iota(jnp.int32, (M, M), 1)
    return jnp.where(line == lane, F32(1), F32(0))


def improved(inverse_ref, g, error, goal):
    twice = 2.0 * identity()

    def more(error):
        return jnp.max(error) > goal

    def step(error):
        gain = 2.0 / (2.0 - error * error)
        pieces = split2(inverse_ref[...])
        rest = twice - dot_pieces(g, pieces)
        inverse_ref[...] = gain * mirrored_product(pieces, split2(rest))
        return error * error * 0.5 * gain

    return lax.while_loop(more, step, error)


def polish_kernel(after_ref, gram_ref, start_ref, inverse_ref):
    x = start_ref[...]
    rest = identity() - dot_pieces(split3(gram_ref[...]), split3(x))
    low = rest.astype(BF16)
    rest = rest + dot(low, low)
    inverse_ref[...] = x + dot_pieces(split2(x), split2(rest))


def finish_kernel(inverse_ref, mine_ref, other_ref, z_hbm, coef_hbm, fitted_hbm, cross_ref, coef_ref, z, fitted, sems):
    n = z.shape[0]
    lines = z.shape[1]
    spans = [pl.ds(k * lines, lines) for k in range(n)]
    copies = copied([(z_hbm.at[span], z.at[k]) for k, span in enumerate(spans)], sems)
    x = split2(inverse_ref[...])
    across = M // TILE
    core = lax.axis_index("c")
    turn = mine_ref.shape[1]
    for r in range(2 * mine_ref.shape[0]):
        i, j = divmod(r, across)
        for k in range(turn):
            first = k * (M // turn) + 8 * i
            tile = jnp.where(core == r % 2, mine_ref[r // 2, k], other_ref[r // 2, k])
            cross_ref[first : first + 8, TILE * j : TILE * (j + 1)] = tile
    coef = dot_pieces(x, split2(cross_ref[...]), 1)
    coef_ref[...] = coef
    outs = [pltpu.make_async_copy(coef_ref, coef_hbm, sems.at[2 * n])]
    outs[0].start()
    low = coef.astype(BF16)
    for k, span in enumerate(spans):
        copies[k].wait()
        fitted[k] = dot(z[k], low)
        out = pltpu.make_async_copy(fitted.at[k], fitted_hbm.at[span], sems.at[n + k])
        out.start()
        outs.append(out)
    for out in outs:
        out.wait()


def cost(us):
    return pl.CostEstimate(flops=int(us * 1.15e9), transcendentals=0, bytes_accessed=0)


def params(mib=48):
    return pltpu.CompilerParams(vmem_limit_bytes=mib * MIB)


def full(shape):
    return pl.BlockSpec(shape, lambda *_: (0,) * len(shape))


def shaped(shape, dtype=F32):
    return jax.ShapeDtypeStruct(shape, dtype)


HBM = pl.BlockSpec(memory_space=pltpu.HBM)
VMEM = pl.BlockSpec(memory_space=pltpu.VMEM)


def in_hbm(array):
    return pltpu.with_memory_space_constraint(array, pltpu.HBM)


def own_part(table, seeds, phases, x, t, turn):
    own, cols = x.shape[1], t.shape[0]
    wide = M // turn
    ins = (table, seeds, phases, x)

    def kernel(*refs):
        own_kernel(turn, *refs)

    return pl.pallas_call(
        kernel,
        in_specs=[HBM] * 5,
        out_specs=[VMEM, VMEM, VMEM, HBM],
        out_shape=[shaped((112, M), BF16), shaped((wide, 112), BF16), shaped((cols + wide, M)), pltpu.HBM((own, M), BF16)],
        scratch_shapes=[pltpu.VMEM(a.shape, a.dtype) for a in ins]
        + [pltpu.VMEM((own, M), BF16), pltpu.VMEM((cols + wide, own), BF16), pltpu.SemaphoreType.DMA((6,))],
        compiler_params=params(),
        cost_estimate=cost(5),
        name="own_part",
    )(*(in_hbm(a) for a in ins), in_hbm(t))


def more_part(shifts, freqs, panel, before, xs, t, turn, tiled=False):
    own, cols = xs[0].shape[1], t.shape[0]
    n = len(xs)
    lines = before.shape[0]
    out = (cols * M // (8 * TILE), 8 * lines // cols, TILE) if tiled else before.shape

    def kernel(*refs):
        more_kernel(shifts, tiled, turn, *refs)

    return pl.pallas_call(
        kernel,
        in_specs=[VMEM, VMEM, VMEM, HBM] + [VMEM] * n,
        out_specs=VMEM,
        out_shape=shaped(out),
        scratch_shapes=[
            pltpu.VMEM((n, lines, own), BF16),
            pltpu.VMEM((own, M), BF16),
            pltpu.SemaphoreType.DMA((n,)),
        ],
        compiler_params=params(),
        cost_estimate=cost(2.6 * n),
        name="more_part",
    )(freqs, panel, before, in_hbm(t), *xs)


def spread(parts, copies):
    return pl.pallas_call(
        spread_kernel,
        in_specs=[VMEM],
        out_specs=VMEM,
        out_shape=shaped((copies, *parts.shape[1:])),
        compiler_params=params(),
        cost_estimate=cost(1),
        name="spread",
    )(parts)


def packed(parts, rows):
    return pl.pallas_call(
        pack_kernel,
        in_specs=[VMEM],
        out_specs=[VMEM, VMEM],
        out_shape=[shaped((rows // 2, PANELS, 8, TILE)), shaped((rows // 2, parts.shape[0], 8, TILE))],
        compiler_params=params(),
        cost_estimate=cost(1),
        name="packed",
    )(parts)


def inverted(mine, other, count):
    def kernel(*refs):
        inverse_kernel(1.0 / count, *refs)

    return pl.pallas_call(
        kernel,
        in_specs=[VMEM, VMEM],
        out_specs=[VMEM] * 3,
        out_shape=[shaped((M, M))] * 2 + [shaped((8, TILE))],
        compiler_params=params(),
        cost_estimate=cost(9),
        name="inverted",
    )(mine, other)


def polished(after, gram, start):
    return pl.pallas_call(
        polish_kernel,
        in_specs=[pl.BlockSpec(memory_space=pl.ANY)] + [VMEM] * 2,
        out_specs=VMEM,
        out_shape=shaped((M, M)),
        compiler_params=params(),
        cost_estimate=cost(5),
        name="polished",
    )(after, gram, start)


def finished(inverse, mine, other, z):
    own = z.shape[0]
    n = 4
    lines = own // n

    return pl.pallas_call(
        finish_kernel,
        in_specs=[VMEM, VMEM, VMEM, HBM],
        out_specs=[HBM, HBM],
        out_shape=[shaped((M, M)), shaped((own, M))],
        scratch_shapes=[
            pltpu.VMEM((M, M), F32),
            pltpu.VMEM((M, M), F32),
            pltpu.VMEM((n, lines, M), BF16),
            pltpu.VMEM((n, lines, M), F32),
            pltpu.SemaphoreType.DMA((2 * n + 1,)),
        ],
        compiler_params=params(),
        cost_estimate=cost(4),
        name="finished",
    )(inverse, mine, other, in_hbm(z))


def exchanged(array, axes):
    return lax.all_to_all(array, axes, 0, 0, tiled=True)


def body(samples, freq_table, feature_seeds, phases, treatment_features):
    count = samples.shape[0] * lax.axis_size(ROWS) * lax.axis_size("z")
    turn = lax.axis_size("z")
    rows = lax.axis_size(ROWS)
    x = samples.T
    t = treatment_features.T

    half = turn // 2

    def moved(block, by):
        return lax.ppermute(block, "z", [(k, (k + by) % turn) for k in range(turn)])

    right = {1: moved(x, 1), 2: moved(x, 2)}
    left = {1: moved(x, -1), 2: moved(x, -2)}
    right[3], left[3], right[half] = moved(right[2], 1), moved(left[2], -1), moved(right[2], half - 2)

    freqs, panel, total, z = own_part(freq_table.T, feature_seeds[None, :], phases[None, :], x, t, turn)
    near = (right[1], left[1], right[2], left[2])
    total = more_part((-1, 1, -2, 2), freqs, panel, total, near, t, turn)
    far = (right[3], left[3], right[half])
    total = more_part((-3, 3, -half), freqs, panel, total, far, t, turn, tiled=True)
    parts = exchanged(spread(exchanged(total, ROWS), turn), "z")
    gram, cross = packed(parts, rows)
    gram = exchanged(gram, ROWS[:2])
    *start, scale = inverted(gram, swapped(gram), count)
    cross = exchanged(cross, ROWS[:2]) * scale
    inverse = polished(cross, *start)
    return finished(inverse, cross, swapped(cross), z)


def swapped(array):
    return lax.ppermute(array, "c", [(0, 1), (1, 0)])


def solution(mesh):
    turn = mesh.shape["rhs"]
    torus = Mesh(mesh.devices.reshape(4, 4, 2, turn), ALL)
    placed = (P(ALL, None), P(), P(), P(), P(ROWS, "z"))
    return jax.shard_map(body, mesh=torus, in_specs=placed, out_specs=(P(), P(ALL, None)), check_vma=False)
```
